32 devices in a mesh: fsdp: 4 (over x, core), seq: 8 (over z, y).
Axes of the slice: x: 2, y: 2, z: 4, core: 2. Of those that a mesh axis runs over, the one named last changes fastest.
Arguments:
- tokens: bfloat16 [4, 56, 28, 512], P('fsdp', 'seq'), may hold values from -6 to 6
- cotangent: bfloat16 [4, 56, 28, 512], P('fsdp', 'seq'), may hold values from -6 to 6
- region_ids: int32 [56, 28], replicated, may hold values from 0 to 3
- relative_index: int32 [49, 49], replicated, may hold values from 0 to 168, as said below
- first_gain: bfloat16 [512], P('fsdp'), may hold values from 0.5 to 1.5
- first_offset: bfloat16 [512], P('fsdp'), may hold values from -3 to 3
- qkv_weight: bfloat16 [512, 1536], P('fsdp'), may hold values from -0.25 to 0.25
- proj_weight: bfloat16 [512, 512], P('fsdp'), may hold values from -0.75 to 0.75
- bias_table: bfloat16 [16, 169], P('fsdp'), may hold values from -4 to 4
- second_gain: bfloat16 [512], P('fsdp'), may hold values from 0.5 to 1.5
- second_offset: bfloat16 [512], P('fsdp'), may hold values from -3 to 3
- expand_weight: bfloat16 [512, 2048], P('fsdp'), may hold values from -0.25 to 0.25
- reduce_weight: bfloat16 [2048, 512], P('fsdp'), may hold values from -0.125 to 0.125
Outputs:
- output: bfloat16 [4, 56, 28, 512], P('fsdp', 'seq')
- tokens_grad: float32 [4, 56, 28, 512], P('fsdp', 'seq')
- first_gain_grad: float32 [512], P('fsdp')
- first_offset_grad: float32 [512], P('fsdp')
- qkv_weight_grad: float32 [512, 1536], P('fsdp')
- proj_weight_grad: float32 [512, 512], P('fsdp')
- bias_table_grad: float32 [16, 169], P('fsdp')
- second_gain_grad: float32 [512], P('fsdp')
- second_offset_grad: float32 [512], P('fsdp')
- expand_weight_grad: float32 [512, 2048], P('fsdp')
- reduce_weight_grad: float32 [2048, 512], P('fsdp')
The draws below stay inside these ranges and needn't reach their ends.
Inputs may be any that keep to these rules, and one draw needn't show every extreme that they name: relative_index[i, j] depends only on the row and column offsets between positions i and j of a 7 x 7 window, and distinct offsets give distinct entries.
All inputs are finite; a program needn't handle non-finite values.
Results may differ from the reference program's by a relative error of at most 0.018.
Values may be sent and summed in bfloat16 or wider, within the bound.
A program may use at most 128 MiB of HBM per device.

```python
import jax
import jax.numpy as jnp
from jax import lax

C = 512
NH = 16
FF = 2048
HD = 32
WS = 7
SHIFT = 3
RELS = 169
IMAGES = 4
HGT = 56
WID = 28


def draw_relative_index(key, part):
    labels = jax.random.permutation(key, (2 * WS - 1) ** 2).astype(jnp.int32)
    places = jnp.arange(WS * WS, dtype=jnp.int32)
    row_of = places // WS
    col_of = places % WS
    offsets = (row_of[:, None] - row_of[None, :] + WS - 1) * (2 * WS - 1) + (col_of[:, None] - col_of[None, :] + WS - 1)
    return labels[offsets].astype(jnp.int32)


def touch_ends(values, stream_key, smallest, largest):
    dims = values.shape
    spot = [jax.random.randint(jax.random.fold_in(stream_key, axis), (), 0, dims[axis]) for axis in range(len(dims))]
    values = values.at[tuple(spot)].set(smallest)
    longest = dims.index(max(dims))
    spot[longest] = (spot[longest] + 1) % dims[longest]
    return values.at[tuple(spot)].set(largest)


def level_of(own_key, shape, cuts, smallest, high):
    loudness, own = 1.0, jax.random.fold_in(own_key, 6)
    for axis_at, shards_of in cuts:
        steps = jnp.exp(jax.random.uniform(jax.random.fold_in(own, axis_at), (shards_of,), jnp.float32, smallest / len(cuts), high / len(cuts)))
        loudness = loudness * jnp.repeat(steps, shape[axis_at] // shards_of).reshape([-1 if axis == axis_at else 1 for axis in range(len(shape))])
    return loudness


def noise(own_key, dims, spread, limit, shards=(), kind=jnp.bfloat16):
    factor_of = level_of(own_key, dims, shards, -0.22, 0.18) if shards else 1.0
    values = jax.random.normal(own_key, dims, jnp.float32) * spread * factor_of
    return jnp.minimum(jnp.maximum(values, -limit), limit).astype(kind)


def setup_inputs(seed: int = 0) -> dict:
    streams_of = jax.random.split(jax.random.key(seed), 14)
    tokens = noise(streams_of[0], (IMAGES, HGT, WID, C), 1.0, 6.0, ((0, 4), (1, 8)))
    cotangent = noise(streams_of[1], (IMAGES, HGT, WID, C), 1.0, 6.0, ((0, 4), (1, 8)))
    region_ids = touch_ends(jax.random.randint(streams_of[2], (HGT, WID), 0, 4), jax.random.fold_in(streams_of[2], 1), 0, 3).astype(jnp.int32)
    relative_index = draw_relative_index(jax.random.fold_in(streams_of[13], 71), 0)
    first_gain = jnp.clip(1.0 + 0.1 * jax.random.normal(streams_of[4], (C,), jnp.float32), 0.5, 1.5).astype(jnp.bfloat16)
    first_offset = noise(streams_of[5], (C,), 0.5, 3.0, ((0, 4),))
    qkv_weight = noise(streams_of[6], (C, 3 * C), C ** -0.5, 0.25, ((0, 4),))
    proj_weight = noise(streams_of[7], (C, C), (C // 8) ** -0.5, 0.75, ((0, 4),))
    bias_table = noise(streams_of[8], (NH, RELS), 1.0, 4.0, ((0, 4),))
    second_gain = jnp.clip(1.0 + 0.1 * jax.random.normal(streams_of[9], (C,), jnp.float32), 0.5, 1.5).astype(jnp.bfloat16)
    second_offset = noise(streams_of[10], (C,), 0.5, 3.0, ((0, 4),))
    expand_weight = noise(streams_of[11], (C, FF), C ** -0.5, 0.25, ((0, 4),))
    reduce_weight = noise(streams_of[12], (FF, C), FF ** -0.5, 0.125, ((0, 4),))
    return {"tokens": tokens, "cotangent": cotangent, "region_ids": region_ids, "relative_index": relative_index, "first_gain": first_gain, "first_offset": first_offset, "qkv_weight": qkv_weight, "proj_weight": proj_weight, "bias_table": bias_table, "second_gain": second_gain, "second_offset": second_offset, "expand_weight": expand_weight, "reduce_weight": reduce_weight}


EPSILON = 1e-05
MASKED = -100.0
SQRT_HALF = 0.7071067811865476
INV_ROOT_TAU = 0.3989422804014327

def layer_norm(values, norm_gain, norm_offset):
    average = lax.optimization_barrier(jnp.mean(values, axis=-1, keepdims=True))
    centred = values - average
    variance = lax.optimization_barrier(jnp.mean(centred * centred, axis=-1, keepdims=True))
    inverse = lax.rsqrt(variance + EPSILON)
    normed = centred * inverse
    return (normed * norm_gain + norm_offset, normed, inverse)

def norm_back(upstream, normed, inverse, norm_gain):
    scaled = upstream * norm_gain
    mean_grad = lax.optimization_barrier(jnp.mean(scaled, axis=-1, keepdims=True))
    second = lax.optimization_barrier(jnp.mean(scaled * normed, axis=-1, keepdims=True))
    grad_in = inverse * (scaled - mean_grad - normed * second)
    lead_axes = tuple(range(upstream.ndim - 1))
    return (grad_in, lax.optimization_barrier(jnp.sum(upstream * normed, axis=lead_axes)), lax.optimization_barrier(jnp.sum(upstream, axis=lead_axes)))

def gelu_parts(hidden):
    normal_cdf = 0.5 * (1.0 + jax.scipy.special.erf(hidden * SQRT_HALF))
    density = jnp.exp(-0.5 * hidden * hidden) * INV_ROOT_TAU
    return (hidden * normal_cdf, normal_cdf + hidden * density)

def widen(low_array):
    return lax.optimization_barrier(low_array).astype(jnp.float32)

def tile_image(field_in):
    lead_count = field_in.shape[2]
    pieces = field_in.reshape(HGT // WS, WS, WID // WS, WS, lead_count, NH, HD)
    return pieces.transpose(4, 0, 2, 5, 1, 3, 6).reshape(lead_count, HGT // WS, WID // WS, NH, WS * WS, HD)

def untile_image(window_tiles):
    lead_count = window_tiles.shape[0]
    pieces = window_tiles.reshape(lead_count, HGT // WS, WID // WS, NH, WS, WS, HD)
    return pieces.transpose(1, 4, 2, 5, 0, 3, 6).reshape(HGT, WID, lead_count, C)

def reference(tokens, cotangent, region_ids, relative_index, first_gain, first_offset, qkv_weight, proj_weight, bias_table, second_gain, second_offset, expand_weight, reduce_weight):
    gain_one = first_gain.astype(jnp.float32)
    offset_one = first_offset.astype(jnp.float32)
    gain_two = second_gain.astype(jnp.float32)
    offset_two = second_offset.astype(jnp.float32)
    query_scale = HD ** (-0.5)
    factors = jnp.array([query_scale, 1.0, 1.0], dtype=jnp.float32)[:, None]
    rel_bias = bias_table.astype(jnp.float32)[:, relative_index]
    region_tiles = region_ids.reshape(HGT // WS, WS, WID // WS, WS).transpose(0, 2, 1, 3).reshape(HGT // WS, WID // WS, WS * WS)
    mask_add = jnp.where(region_tiles[..., :, None] == region_tiles[..., None, :], 0.0, MASKED).astype(jnp.float32)[:, :, None]

    def one_image(totals, items):
        image, image_cot = items
        inputs = image.astype(jnp.float32)
        normed_one, hat_one, inv_one = layer_norm(inputs, gain_one, offset_one)
        first_low = normed_one.astype(jnp.bfloat16).reshape(-1, C)
        qkv_all = jnp.dot(first_low, qkv_weight, preferred_element_type=jnp.float32).reshape(HGT, WID, 3, C)
        qkv_low = (qkv_all * factors).astype(jnp.bfloat16)
        qkv_tiles = widen(tile_image(jnp.roll(qkv_low, (-SHIFT, -SHIFT), axis=(0, 1))))
        queries, key_tiles, value_tiles = (qkv_tiles[0], qkv_tiles[1], qkv_tiles[2])
        scores = jnp.einsum('xyhid,xyhjd->xyhij', queries, key_tiles) + rel_bias + mask_add
        exp_scores = jnp.exp(scores)
        row_total = lax.optimization_barrier(jnp.sum(exp_scores, axis=-1, keepdims=True))
        log_total = jnp.log(row_total)
        attn_probs = widen((exp_scores / row_total).astype(jnp.bfloat16))
        attn_tiles = jnp.einsum('xyhij,xyhjd->xyhid', attn_probs, value_tiles).astype(jnp.bfloat16)
        attended = jnp.roll(untile_image(attn_tiles[None])[:, :, 0], (SHIFT, SHIFT), axis=(0, 1)).reshape(-1, C)
        middle = inputs + jnp.dot(attended, proj_weight, preferred_element_type=jnp.float32).reshape(HGT, WID, C)
        normed_two, hat_two, inv_two = layer_norm(middle, gain_two, offset_two)
        second_low = normed_two.astype(jnp.bfloat16).reshape(-1, C)
        hidden = jnp.dot(second_low, expand_weight, preferred_element_type=jnp.float32)
        activated, slope = gelu_parts(hidden)
        act_low = activated.astype(jnp.bfloat16)
        output = (middle + jnp.dot(act_low, reduce_weight, preferred_element_type=jnp.float32).reshape(HGT, WID, C)).astype(jnp.bfloat16)
        cot_flat = image_cot.reshape(-1, C)
        reduce_grad = jnp.dot(act_low.T, cot_flat, preferred_element_type=jnp.float32)
        hidden_grad = (jnp.dot(cot_flat, reduce_weight.T, preferred_element_type=jnp.float32) * slope).astype(jnp.bfloat16)
        expand_grad = jnp.dot(second_low.T, hidden_grad, preferred_element_type=jnp.float32)
        upstream_two = jnp.dot(hidden_grad, expand_weight.T, preferred_element_type=jnp.float32).reshape(HGT, WID, C)
        back_two, gain_two_grad, offset_two_grad = norm_back(upstream_two, hat_two, inv_two, gain_two)
        middle_grad = image_cot.astype(jnp.float32) + back_two
        middle_low = middle_grad.astype(jnp.bfloat16).reshape(-1, C)
        proj_grad = jnp.dot(attended.T, middle_low, preferred_element_type=jnp.float32)
        attended_grad = jnp.dot(middle_low, proj_weight.T, preferred_element_type=jnp.float32).astype(jnp.bfloat16).reshape(HGT, WID, 1, C)
        grad_tiles = widen(tile_image(jnp.roll(attended_grad, (-SHIFT, -SHIFT), axis=(0, 1))))[0]
        probs_back = jnp.exp(scores - log_total)
        probs_low = widen(probs_back.astype(jnp.bfloat16))
        value_grad = jnp.einsum('xyhij,xyhid->xyhjd', probs_low, grad_tiles)
        prob_grad = jnp.einsum('xyhid,xyhjd->xyhij', grad_tiles, value_tiles)
        score_grad = probs_back * (prob_grad - lax.optimization_barrier(jnp.sum(probs_back * prob_grad, axis=-1, keepdims=True)))
        score_low = widen(score_grad.astype(jnp.bfloat16))
        query_grad = jnp.einsum('xyhij,xyhjd->xyhid', score_low, key_tiles) * query_scale
        key_grad = jnp.einsum('xyhij,xyhid->xyhjd', score_low, queries)
        stacked = jnp.stack([query_grad, key_grad, value_grad]).astype(jnp.bfloat16)
        qkv_grad = jnp.roll(untile_image(stacked), (SHIFT, SHIFT), axis=(0, 1)).reshape(-1, 3 * C)
        qkv_grad_w = jnp.dot(first_low.T, qkv_grad, preferred_element_type=jnp.float32)
        upstream_one = jnp.dot(qkv_grad, qkv_weight.T, preferred_element_type=jnp.float32).reshape(HGT, WID, C)
        back_one, gain_one_grad, offset_one_grad = norm_back(upstream_one, hat_one, inv_one, gain_one)
        tokens_grad = middle_grad + back_one
        score_sum = lax.optimization_barrier(jnp.sum(score_grad, axis=(0, 1))).reshape(NH, -1)
        table_grad = jax.ops.segment_sum(score_sum.T, relative_index.reshape(-1), num_segments=RELS).T
        terms = (gain_one_grad, offset_one_grad, qkv_grad_w, proj_grad, table_grad, gain_two_grad, offset_two_grad, expand_grad, reduce_grad)
        return (tuple((total + term for total, term in zip(totals, terms))), (output, tokens_grad))
    start = (jnp.zeros((C,), jnp.float32), jnp.zeros((C,), jnp.float32), jnp.zeros((C, 3 * C), jnp.float32), jnp.zeros((C, C), jnp.float32), jnp.zeros((NH, RELS), jnp.float32), jnp.zeros((C,), jnp.float32), jnp.zeros((C,), jnp.float32), jnp.zeros((C, FF), jnp.float32), jnp.zeros((FF, C), jnp.float32))
    sums, per_image = lax.scan(one_image, start, (tokens, cotangent))
    outputs, grads_in = per_image
    return (outputs, grads_in, sums[0], sums[1], sums[2], sums[3], sums[4], sums[5], sums[6], sums[7], sums[8])
```

```python
import functools

import jax
import jax.numpy as jnp
from jax import lax
from jax.experimental import pallas as pl
from jax.experimental.pallas import tpu as pltpu
from jax.sharding import PartitionSpec as P

WS = 7
SHIFT = 3
SLOT = 64
LANES = 256

EPSILON = 1e-05
MASKED = -100.0
REMOVED = -1e30
SQRT_HALF = 0.7071067811865476
INV_ROOT_TAU = 0.3989422804014327

F32 = jnp.float32
LOW = jnp.bfloat16


def dot(left, right, left_dim, right_dim):
    dims = (((left_dim,), (right_dim,)), ((), ()))
    return lax.dot_general(left, right, dims, preferred_element_type=F32)


def nn(left, right):
    return dot(left, right, 1, 0)


def nt(left, right):
    return dot(left, right, 1, 1)


def tn(left, right):
    return dot(left, right, 0, 0)


def iota(shape, dim):
    return lax.broadcasted_iota(jnp.int32, shape, dim)


def split(values):
    high = values.astype(LOW)
    return high, (values - high.astype(F32)).astype(LOW)


def sum_exact(values, ones):
    high, low = split(values)
    both = nn(jnp.concatenate([high, low], axis=0), ones)
    return both[: values.shape[0]] + both[values.shape[0] :]


def layer_norm(values, norm_gain, norm_offset):
    average = jnp.mean(values, axis=-1, keepdims=True)
    centred = values - average
    variance = jnp.mean(centred * centred, axis=-1, keepdims=True)
    inverse = lax.rsqrt(variance + EPSILON)
    normed = centred * inverse
    return normed * norm_gain + norm_offset, normed, inverse


def norm_back(upstream, normed, inverse, norm_gain):
    scaled = upstream * norm_gain
    mean_grad = jnp.mean(scaled, axis=-1, keepdims=True)
    second = jnp.mean(scaled * normed, axis=-1, keepdims=True)
    grad_in = inverse * (scaled - mean_grad - normed * second)
    gain_grad = jnp.sum(upstream * normed, axis=0, keepdims=True)
    return grad_in, gain_grad, jnp.sum(upstream, axis=0, keepdims=True)


def gelu_parts(hidden):
    normal_cdf = 0.5 * (1.0 + lax.erf(hidden * SQRT_HALF))
    density = jnp.exp(-0.5 * hidden * hidden) * INV_ROOT_TAU
    return hidden * normal_cdf, normal_cdf + hidden * density


def place_of(slot_at, num_cols):
    window, spot = slot_at // SLOT, slot_at % SLOT
    across = num_cols // WS
    row_in = sum((spot >= WS * step).astype(jnp.int32) for step in range(1, WS))
    row = (window // across) * WS + row_in
    col = (window % across) * WS + spot - row_in * WS
    return row, col, spot < WS * WS


class Dims:
    def __init__(self, owners, size, num_rows, num_cols, width, hidden, num_heads, entries):
        self.owners, self.size = owners, size
        self.pairs, self.halves = owners // 2, size // 2
        self.num_rows, self.num_cols, self.width = num_rows, num_cols, width
        self.hidden, self.num_heads, self.entries = hidden, num_heads, entries
        self.windows = (num_rows // WS) * (num_cols // WS)
        self.slots = self.windows * SLOT
        self.stride = -(-num_cols // 16) * 16
        self.natural = -(-num_rows * self.stride // 128) * 128
        self.part = width // owners
        self.scatter = self.part % (16 * size) == 0
        self.fine = self.halves if self.scatter else 1
        self.piece = self.part // (2 * self.fine)
        self.tiles = hidden // width
        self.groups = width // LANES
        self.per_group = num_heads // self.groups
        self.head_dim = width // num_heads
        self.chunks = 2 * self.tiles + 4
        pairs, halves = self.pairs, self.halves
        self.copies = 32 + 5 * (3 * pairs - 2) + self.chunks * (pairs + 1 + 2 * (halves - 1))
        self.copies += pairs + size


def body(d, *refs):
    (tok, cot, reg, rel, gain_a, offset_a, gain_b, offset_b, table) = refs[:9]
    weights = refs[9:13]
    (out, tok_grad, d_gain_a, d_offset_a, d_qkv, d_proj, d_table, d_gain_b, d_offset_b, d_expand, d_reduce) = refs[13:24]
    fulls = refs[24:28]
    (small, halo_tok, halo_cot, halo_out, halo_grad, came_grad, natural, hat_a, hat_b, middle, low_a) = refs[28:39]
    (qkv, probs, attended, slope, act, perm, perm_t, heads, ones, onehot, rel_pad, bias, spread, mask) = refs[39:53]
    (at_a, at_a_in, at_b, at_b_in, at_c, at_c_in, at_d, at_d_in, g_cot, g_hid, g_mid, g_qkv) = refs[53:65]
    (grads, in_two, sum_two, in_three, sum_three, in_four, result, small_grad, small_in, small_sum, small_two, small_all, table_sum) = refs[65:78]
    send_sem, recv_sem, copy_sem = refs[78:]

    pairs, halves, size, owners = d.pairs, d.halves, d.size, d.owners
    width, part = d.width, d.part
    place, line = lax.axis_index("fsdp"), lax.axis_index("seq")
    pair, core = place // 2, place % 2
    half, side = line // 2, line % 2
    mesh_id = pl.DeviceIdType.MESH
    partner = {"fsdp": pair * 2 + 1 - core, "seq": line}
    beside = {"fsdp": place, "seq": half * 2 + 1 - side}
    pair_peers = [(pair + step) % pairs for step in range(1, pairs)]
    pair_sources = [(pair + pairs - step) % pairs for step in range(1, pairs)]
    across = [{"fsdp": peer * 2 + core, "seq": line} for peer in pair_peers]
    half_peers = [(half + step) % halves for step in range(1, halves)]
    along = [{"fsdp": place, "seq": peer * 2 + side} for peer in half_peers]
    seq_peers = [{"fsdp": place, "seq": (line + step) % size} for step in range(1, size)]
    later, earlier = seq_peers[0], seq_peers[-1]

    used = [0]
    started = []

    def send(source, target, device):
        slot = used[0]
        used[0] += 1
        copy = pltpu.make_async_remote_copy(
            src_ref=source,
            dst_ref=target,
            send_sem=send_sem.at[slot],
            recv_sem=recv_sem.at[slot],
            device_id=device,
            device_id_type=mesh_id,
        )
        copy.start()
        started.append(copy)
        return copy

    small[place] = jnp.zeros(small.shape[1:], F32)
    for at, vector in enumerate((gain_a, offset_a, gain_b, offset_b)):
        small[place, at : at + 1, :part] = vector[...].astype(F32)
    table_rows = table.shape[0]
    small[place, 4 : 4 + table_rows, : d.entries] = table[...].astype(F32)

    barrier = pltpu.get_barrier_semaphore()
    greeted = [partner] + across + seq_peers
    for device in greeted:
        pl.semaphore_signal(barrier, inc=1, device_id=device, device_id_type=mesh_id)
    pl.semaphore_wait(barrier, len(greeted))

    far, near, home, kept = {}, {}, {}, []

    def gather_far(at):
        for step, device in enumerate(across):
            far[at, step] = send(weights[at].at[side], fulls[at].at[place, side], device)
        home[at] = [send(weights[at], fulls[at].at[place], partner)]
        copy = pltpu.make_async_copy(weights[at], fulls[at].at[place], copy_sem.at[at])
        copy.start()
        home[at].append(copy)

    def gather_near(at):
        for step, source in enumerate(pair_sources):
            far[at, step].wait_recv()
            came = fulls[at].at[source * 2 + core, side]
            near[at, step] = send(came, came, beside)

    def gather_home(at):
        for step, source in enumerate(pair_sources):
            near[at, step].wait_recv()
            came = fulls[at].at[source * 2 + core]
            home[at].append(send(came, came, partner))

    def gather_done(at):
        for index, copy in enumerate(home[at]):
            if index == 1:
                copy.wait()
            else:
                copy.wait_recv()

    own_small = small.at[place]
    small_far = [send(own_small, own_small, device) for device in across]
    small_home = [send(own_small, own_small, partner)]
    halo_copies = [send(tok.at[0, 0:SHIFT], halo_tok, earlier)]
    gather_far(0)
    gather_far(1)
    halo_copies.append(send(cot.at[0, 0:SHIFT], halo_cot, earlier))

    row, col, real = place_of(iota((d.slots, d.natural), 0), d.num_cols)
    token_col = jnp.where(col + SHIFT >= d.num_cols, col + SHIFT - d.num_cols, col + SHIFT)
    hit = (iota((d.slots, d.natural), 1) == row * d.stride + token_col) & real
    perm[...] = jnp.where(hit, 1.0, 0.0).astype(LOW)
    row, col, real = place_of(iota((d.natural, d.slots), 1), d.num_cols)
    token_col = jnp.where(col + SHIFT >= d.num_cols, col + SHIFT - d.num_cols, col + SHIFT)
    hit = (iota((d.natural, d.slots), 0) == row * d.stride + token_col) & real
    perm_t[...] = jnp.where(hit, 1.0, 0.0).astype(LOW)
    span = d.per_group * SLOT
    hit = iota((span, LANES), 0) // SLOT == iota((span, LANES), 1) // d.head_dim
    heads[...] = jnp.where(hit, 1.0, 0.0).astype(LOW)
    hit = iota((span, span), 0) // SLOT == iota((span, span), 1) // SLOT
    ones[...] = jnp.where(hit, 1.0, 0.0).astype(LOW)

    grid_rows, grid_cols = reg.shape
    row, col, real = place_of(iota((d.slots, grid_rows), 0), d.num_cols)
    picked = jnp.where(iota((d.slots, grid_rows), 1) == line * d.num_rows + row, 1.0, 0.0)
    by_row = nn(picked.astype(LOW), reg[...].astype(F32).astype(LOW))
    row, col, real = place_of(iota((d.slots, grid_cols), 0), d.num_cols)
    regions = jnp.sum(
        jnp.where(iota((d.slots, grid_cols), 1) == col, by_row, 0.0), axis=1, keepdims=True
    )
    regions_t = jnp.transpose(jnp.broadcast_to(regions, (d.slots, 128)))
    for window in range(d.windows):
        down = regions[window * SLOT : (window + 1) * SLOT]
        over = regions_t[0:1, window * SLOT : (window + 1) * SLOT]
        added = jnp.where(down == over, 0.0, MASKED).astype(F32)
        mask[window] = jnp.concatenate([added, added], axis=1)

    positions = rel.shape[0]
    rel_pad[...] = jnp.full(rel_pad.shape, -1.0, F32)
    rel_pad[:positions, :positions] = rel[...].astype(F32)
    rel_pad[...] = jnp.transpose(rel_pad[...])
    table_lanes = small.shape[2]

    @pl.loop(0, onehot.shape[0])
    def _(at):
        rel_t = rel_pad[:SLOT]
        column = jnp.sum(
            jnp.where(iota(rel_t.shape, 1) == at, rel_t, 0.0), axis=1, keepdims=True
        )
        hit = column == iota((SLOT, table_lanes), 1).astype(F32)
        onehot[at] = jnp.where(hit, 1.0, 0.0).astype(LOW)

    natural[...] = jnp.zeros(natural.shape, LOW)
    keep = d.num_rows - SHIFT

    def windowed(field, halo, copy):
        copy.wait_recv()
        for at in range(d.num_rows):
            source = field[0, at + SHIFT] if at < keep else halo[at - keep]
            natural[at * d.stride : at * d.stride + d.num_cols] = source
        return nn(perm[...], natural[...])

    inputs = windowed(tok, halo_tok, halo_copies[0])

    for step, source in enumerate(pair_sources):
        small_far[step].wait_recv()
        came = small.at[source * 2 + core]
        small_home.append(send(came, came, partner))
    gather_near(0)
    gather_far(2)
    for copy in small_home:
        copy.wait_recv()

    def vector_of(at):
        return jnp.concatenate([small[owner, at : at + 1, :part] for owner in range(owners)], axis=1)

    norm_gain_a, norm_offset_a, norm_gain_b, norm_offset_b = [vector_of(at) for at in range(4)]
    normed, normed_hat, inverse_a = layer_norm(inputs, norm_gain_a, norm_offset_a)
    hat_a[...] = normed_hat
    low_a[...] = normed.astype(LOW)

    def by_owner(values):
        rows = values.shape[0] // owners
        return values.reshape(pairs, 2, rows, values.shape[1])

    at_a[...] = by_owner(jnp.transpose(low_a[...]))
    swaps = {}
    swaps["a"] = send(at_a.at[:, 1 - core], at_a_in, partner)
    gather_home(0)

    whole_table = jnp.concatenate(
        [small[owner, 4 : 4 + table_rows] for owner in range(owners)], axis=0
    ).astype(LOW)

    @pl.loop(0, positions)
    def _(at):
        spread[pl.ds(at, d.num_heads, stride=SLOT), :SLOT] = nt(whole_table, onehot[at])

    removed = jnp.where(iota((SLOT, SLOT), 1) < WS * WS, 0.0, REMOVED)
    for head in range(0, d.num_heads, 2):
        one = spread[head * SLOT : (head + 1) * SLOT, :SLOT] + removed
        two = spread[(head + 1) * SLOT : (head + 2) * SLOT, :SLOT] + removed
        bias[:, head * SLOT : (head + 2) * SLOT] = jnp.concatenate([one, two], axis=1)

    gather_near(1)
    gather_far(3)
    g_cot[0] = windowed(cot, halo_cot, halo_copies[1]).astype(LOW)
    swaps["cot"] = send(g_cot.at[0], g_cot.at[1], partner)
    gather_done(0)

    def weight(at, cols):
        values = fulls[at][:, :, :, cols]
        return values.reshape(-1, values.shape[-1])

    scale = d.head_dim ** (-0.5)
    for at in range(3):
        columns = pl.ds(at * width, width)
        values = nn(low_a[...], weight(0, columns))
        qkv[at] = (values * scale if at == 0 else values).astype(LOW)
    gather_home(1)

    def span_of(window, group):
        return pl.ds(window * SLOT, SLOT), pl.ds(group * LANES, LANES)

    def blocks_of(tile):
        return jnp.concatenate([tile] * d.per_group, axis=0) * heads[...]

    for window in range(d.windows):
        for group in range(d.groups):
            rows, lanes = span_of(window, group)
            scores = nt(qkv[0, rows, lanes], blocks_of(qkv[1, rows, lanes]))
            scores += bias[:, group * span : (group + 1) * span]
            scores += jnp.concatenate([mask[window]] * (d.per_group // 2), axis=1)
            powers = jnp.exp(scores)
            share = powers / sum_exact(powers, ones[...])
            probs[window, group] = share
            found = nn(share.astype(LOW), blocks_of(qkv[2, rows, lanes]))
            attended[rows, lanes] = found.astype(LOW)
        if window == 0:
            gather_near(2)
    at_c[...] = by_owner(jnp.transpose(attended[...]))
    swaps["c"] = send(at_c.at[:, 1 - core], at_c_in, partner)
    gather_done(1)
    middle[...] = inputs + nn(attended[...], weight(1, slice(None)))
    normed, normed_hat, inverse_b = layer_norm(middle[...], norm_gain_b, norm_offset_b)
    hat_b[...] = normed_hat
    low_b = normed.astype(LOW)
    at_b[...] = by_owner(jnp.transpose(low_b))
    swaps["b"] = send(at_b.at[:, 1 - core], at_b_in, partner)
    gather_home(2)
    gather_near(3)
    gather_done(2)

    tile_owners = owners // d.tiles
    for tile in range(d.tiles):
        columns = pl.ds(tile * width, width)
        hidden = nn(low_b, weight(2, columns))
        activated, slope_tile = gelu_parts(hidden)
        slope[tile] = slope_tile
        act_low = activated.astype(LOW)
        act[:, tile * width : (tile + 1) * width] = act_low
        turned = jnp.transpose(act_low).reshape(tile_owners, -1, d.slots)
        for at in range(tile_owners):
            owner = tile * tile_owners + at
            at_d[owner // 2, owner % 2] = turned[at]
    gather_home(3)
    swaps["d"] = send(at_d.at[:, 1 - core], at_d_in, partner)

    stage_copies = {}

    def reduce_start(chunk, own, came, right, came_right):
        total = nn(own.reshape(-1, d.slots), right) + nn(came.reshape(-1, d.slots), came_right)
        grads[chunk] = total.astype(LOW).reshape(grads.shape[1:])
        stage_copies[chunk, 0] = [
            send(grads.at[chunk, peer], in_two.at[chunk, step], device)
            for step, (peer, device) in enumerate(zip(pair_peers, across))
        ]

    def wide(ref, *index):
        return ref[index].astype(F32)

    def stage_two(chunk):
        total = wide(grads, chunk, pair)
        for step in range(pairs - 1):
            total += wide(in_two, chunk, step)
        sum_two[chunk] = total.astype(LOW)
        return [send(sum_two.at[chunk, 1 - side], in_three.at[chunk], beside)]

    def stage_three(chunk):
        total = (wide(sum_two, chunk, side) + wide(in_three, chunk)).astype(LOW)
        sum_three[chunk] = total
        if d.scatter:
            return [
                send(sum_three.at[chunk, peer], in_four.at[chunk, step], device)
                for step, (peer, device) in enumerate(zip(half_peers, along))
            ]
        in_four[chunk, half] = total[0]
        mine = in_four.at[chunk, half]
        return [send(sum_three.at[chunk, 0], mine, device) for device in along]

    def stage_four(chunk):
        if d.scatter:
            total = wide(sum_three, chunk, half)
            for step in range(halves - 1):
                total += wide(in_four, chunk, step)
            result[chunk, side, half] = total.astype(LOW)
            mine = result.at[chunk, side, half]
            return [send(mine, mine, device) for device in along]
        total = wide(in_four, chunk, 0)
        for at in range(1, halves):
            total += wide(in_four, chunk, at)
        result[chunk, side, 0] = total.astype(LOW)
        return []

    def stage_five(chunk):
        mine = result.at[chunk, side]
        return [send(mine, mine, beside)]

    def stage_six(chunk):
        total = wide(result, chunk).reshape(part, width)
        if chunk < d.tiles:
            d_reduce[chunk * part : (chunk + 1) * part] = total
        elif chunk < 2 * d.tiles:
            at = chunk - d.tiles
            d_expand[:, at * width : (at + 1) * width] = total
        elif chunk == 2 * d.tiles:
            d_proj[...] = total
        else:
            at = chunk - 2 * d.tiles - 1
            d_qkv[:, at * width : (at + 1) * width] = total
        return []

    stages = (stage_two, stage_three, stage_four, stage_five, stage_six)
    events = sorted(
        (chunk + lag, -lag, chunk) for chunk in range(d.chunks) for lag in range(len(stages))
    )

    def advance(limit):
        while events and events[0][0] <= limit:
            _, lag, chunk = events.pop(0)
            for copy in stage_copies[chunk, -lag]:
                copy.wait_recv()
            stage_copies[chunk, 1 - lag] = stages[-lag](chunk)

    swaps["cot"].wait_recv()
    swaps["d"].wait_recv()
    for chunk in range(d.tiles):
        rows = pl.ds(chunk * part, part)
        reduce_start(chunk, at_d[:, core, rows], at_d_in[:, rows], g_cot[0], g_cot[1])

    gather_done(3)
    for tile in range(d.tiles):
        whole = fulls[3][tile * tile_owners : (tile + 1) * tile_owners].reshape(width, width)
        hidden_grad = (nt(g_cot[0], whole) * slope[tile]).astype(LOW)
        g_hid[tile, 0] = hidden_grad
        swaps["h", tile] = send(g_hid.at[tile, 0], g_hid.at[tile, 1], partner)
        term = nt(hidden_grad, weight(2, pl.ds(tile * width, width)))
        upstream_two = term if tile == 0 else upstream_two + term
    advance(0)

    swaps["b"].wait_recv()
    for tile in range(d.tiles):
        swaps["h", tile].wait_recv()
        reduce_start(d.tiles + tile, at_b[:, core], at_b_in[...], g_hid[tile, 0], g_hid[tile, 1])

    out_tiles = (middle[...] + nn(act[...], fulls[3][...].reshape(-1, width))).astype(LOW)
    out_rows = nn(perm_t[...], out_tiles).astype(LOW)
    for at in range(d.num_rows):
        field = out_rows[at * d.stride : at * d.stride + d.num_cols]
        if at < keep:
            out[0, at + SHIFT] = field
        else:
            halo_out[at - keep] = field
    last = [send(halo_out, out.at[0, 0:SHIFT], later)]

    back_two, gain_b_grad, offset_b_grad = norm_back(upstream_two, hat_b[...], inverse_b, norm_gain_b)
    middle_grad = g_cot[0].astype(F32) + back_two
    middle_low = middle_grad.astype(LOW)
    g_mid[0] = middle_low
    swaps["m"] = send(g_mid.at[0], g_mid.at[1], partner)
    attended[...] = nt(middle_low, weight(1, slice(None))).astype(LOW)
    middle[...] = middle_grad
    swaps["m"].wait_recv()
    swaps["c"].wait_recv()
    reduce_start(2 * d.tiles, at_c[:, core], at_c_in[...], g_mid[0], g_mid[1])
    advance(1)

    def fold(values):
        kept_lanes = values * heads[...].astype(F32)
        return jnp.sum(kept_lanes.reshape(d.per_group, SLOT, LANES), axis=0)

    for window in range(d.windows):
        for group in range(d.groups):
            rows, lanes = span_of(window, group)
            query, key, value = [qkv[at, rows, lanes] for at in range(3)]
            keys = blocks_of(key)
            share = probs[window, group]
            given = attended[rows, lanes]
            prob_grad = nt(given, blocks_of(value))
            inner = sum_exact(share * prob_grad, ones[...])
            score_grad = share * (prob_grad - inner)
            score_low = score_grad.astype(LOW)
            across_heads = slice(group * span, (group + 1) * span)
            if window == 0:
                bias[:, across_heads] = score_grad
            else:
                bias[:, across_heads] += score_grad
            g_qkv[0, 0, rows, lanes] = (nn(score_low, keys) * scale).astype(LOW)
            g_qkv[1, 0, rows, lanes] = fold(tn(score_low, query)).astype(LOW)
            g_qkv[2, 0, rows, lanes] = fold(tn(share.astype(LOW), given)).astype(LOW)
        advance(2 + window)

    for at in range(3):
        swaps["q", at] = send(g_qkv.at[at, 0], g_qkv.at[at, 1], partner)
    swaps["a"].wait_recv()
    for at in range(3):
        term = nt(g_qkv[at, 0], weight(0, pl.ds(at * width, width)))
        upstream_one = term if at == 0 else upstream_one + term
        swaps["q", at].wait_recv()
        reduce_start(2 * d.tiles + 1 + at, at_a[:, core], at_a_in[...], g_qkv[at, 0], g_qkv[at, 1])
    advance(6)

    back_one, gain_a_grad, offset_a_grad = norm_back(upstream_one, hat_a[...], inverse_a, norm_gain_a)

    for head in range(d.num_heads):
        spread[head * SLOT : (head + 1) * SLOT, :SLOT] = bias[:, head * SLOT : (head + 1) * SLOT]

    batch = LANES // SLOT

    for step in range(onehot.shape[0] // batch):
        pieces = [
            spread[pl.ds(step * batch + at, d.num_heads, stride=SLOT), :SLOT] for at in range(batch)
        ]
        high, low = split(jnp.concatenate(pieces, axis=1))
        picks = onehot[pl.ds(step * batch, batch)].reshape(batch * SLOT, table_lanes)
        table_sum[step] = nn(jnp.concatenate([high, low], axis=0), picks)

    table_total = jnp.sum(table_sum[...], axis=0)
    table_grad = table_total[: d.num_heads] + table_total[d.num_heads :]
    small_grad[...] = jnp.zeros(small_grad.shape, F32)
    vector_grads = (gain_a_grad, offset_a_grad, gain_b_grad, offset_b_grad)
    for owner in range(owners):
        spot = (owner // 2, owner % 2)
        for at, vector in enumerate(vector_grads):
            small_grad[spot + (slice(at, at + 1), slice(0, part))] = vector[:, owner * part : (owner + 1) * part]
        rows = table_grad[owner * table_rows : (owner + 1) * table_rows]
        small_grad[spot + (slice(4, 4 + table_rows),)] = rows
    small_home = send(small_grad.at[:, 1 - core], small_in, partner)
    advance(7)

    final = middle[...] + back_one
    high, low = split(final)
    final_rows = nn(perm_t[...], high) + nn(perm_t[...], low)
    for at in range(d.num_rows):
        field = final_rows[at * d.stride : at * d.stride + d.num_cols]
        if at < keep:
            tok_grad[0, at + SHIFT] = field
        else:
            halo_grad[at - keep] = field.astype(LOW)
    grad_copy = send(halo_grad, came_grad, later)

    small_home.wait_recv()
    small_sum[...] = small_grad[:, core] + small_in[...]
    small_far = [
        send(small_sum.at[peer], small_two.at[step], device)
        for step, (peer, device) in enumerate(zip(pair_peers, across))
    ]
    advance(8)
    total = small_sum[pair]
    for step in range(pairs - 1):
        small_far[step].wait_recv()
        total += small_two[step]
    small_all[line] = total
    mine = small_all.at[line]
    small_copies = [send(mine, mine, device) for device in seq_peers]
    advance(9)
    grad_copy.wait_recv()
    for at in range(SHIFT):
        tok_grad[0, at] = came_grad[at].astype(F32)
    for copy in small_copies:
        copy.wait_recv()
    total = small_all[0]
    for at in range(1, size):
        total += small_all[at]
    for at, target in enumerate((d_gain_a, d_offset_a, d_gain_b, d_offset_b)):
        target[...] = total[at : at + 1, :part]
    d_table[...] = total[4 : 4 + table_rows, : d.entries]
    advance(d.chunks + len(stages))

    for copy in last:
        copy.wait_recv()
    for copy in started:
        copy.wait_send()


def shards(
    tokens,
    cotangent,
    region_ids,
    relative_index,
    first_gain,
    first_offset,
    qkv_weight,
    proj_weight,
    bias_table,
    second_gain,
    second_offset,
    expand_weight,
    reduce_weight,
):
    owners = lax.axis_size("fsdp")
    size = lax.axis_size("seq")
    _, num_rows, num_cols, width = tokens.shape
    table_rows, entries = bias_table.shape
    hidden = expand_weight.shape[1]
    num_heads = table_rows * owners
    d = Dims(owners, size, num_rows, num_cols, width, hidden, num_heads, entries)
    pairs, halves, part = d.pairs, d.halves, d.part
    slots, span = d.slots, d.per_group * SLOT
    weights = [
        weight.reshape(2, weight.shape[0] // 2, weight.shape[1])
        for weight in (qkv_weight, proj_weight, expand_weight, reduce_weight)
    ]
    vectors = [
        vector.reshape(1, part) for vector in (first_gain, first_offset, second_gain, second_offset)
    ]
    entry_lanes = -(-entries // 128) * 128
    small_rows = -(-(4 + table_rows) // 8) * 8
    held = -(-WS * WS // 4) * 4
    chunks, fine, piece = d.chunks, d.fine, d.piece
    hidden_part = hidden // owners

    def low(*shape):
        return pltpu.VMEM(shape, LOW)

    def full(*shape):
        return pltpu.VMEM(shape, F32)

    scratch = [low(owners, *weight.shape) for weight in weights]
    scratch += [
        full(owners, small_rows, entry_lanes),
        low(SHIFT, num_cols, width),
        low(SHIFT, num_cols, width),
        low(SHIFT, num_cols, width),
        low(SHIFT, num_cols, width),
        low(SHIFT, num_cols, width),
        low(d.natural, width),
        full(slots, width),
        full(slots, width),
        full(slots, width),
        low(slots, width),
    ]
    scratch += [
        low(3, slots, width),
        full(d.windows, d.groups, SLOT, span),
        low(slots, width),
        full(d.tiles, slots, width),
        low(slots, hidden),
        low(slots, d.natural),
        low(d.natural, slots),
        low(span, LANES),
        low(span, span),
        low(held, SLOT, entry_lanes),
        full(128, 128),
        full(SLOT, num_heads * SLOT),
        full(num_heads * SLOT, 128),
        full(d.windows, SLOT, 2 * SLOT),
    ]
    for rows in (part, part, part, hidden_part):
        scratch += [low(pairs, 2, rows, slots), low(pairs, rows, slots)]
    scratch += [
        low(2, slots, width),
        low(d.tiles, 2, slots, width),
        low(2, slots, width),
        low(3, 2, slots, width),
    ]
    scratch += [
        low(chunks, pairs, 2, fine, piece, width),
        low(chunks, max(pairs - 1, 1), 2, fine, piece, width),
        low(chunks, 2, fine, piece, width),
        low(chunks, fine, piece, width),
        low(chunks, fine, piece, width),
        low(chunks, halves, piece, width),
        low(chunks, 2, fine, piece, width),
        full(pairs, 2, small_rows, entry_lanes),
        full(pairs, small_rows, entry_lanes),
        full(pairs, small_rows, entry_lanes),
        full(max(pairs - 1, 1), small_rows, entry_lanes),
        full(size, small_rows, entry_lanes),
        full(held * SLOT // LANES, 2 * num_heads, entry_lanes),
    ]
    scratch += [pltpu.SemaphoreType.DMA((d.copies,))] * 2 + [pltpu.SemaphoreType.DMA((4,))]

    def shape(*dims):
        return jax.ShapeDtypeStruct(dims, F32)

    in_vmem = pl.BlockSpec(memory_space=pltpu.VMEM)
    outs = pl.pallas_call(
        functools.partial(body, d),
        out_shape=[
            jax.ShapeDtypeStruct(tokens.shape, LOW),
            shape(*tokens.shape),
            shape(1, part),
            shape(1, part),
            shape(part, 3 * width),
            shape(part, width),
            shape(table_rows, entries),
            shape(1, part),
            shape(1, part),
            shape(part, hidden),
            shape(hidden_part, width),
        ],
        in_specs=[in_vmem] * 9 + [pl.BlockSpec(memory_space=pl.ANY)] * 4,
        out_specs=[in_vmem] * 11,
        scratch_shapes=scratch,
        compiler_params=pltpu.CompilerParams(
            collective_id=0, has_side_effects=True, vmem_limit_bytes=60 * 1024 * 1024
        ),
    )(tokens, cotangent, region_ids, relative_index, *vectors, bias_table, *weights)
    outs = list(outs)
    for at in (2, 3, 7, 8):
        outs[at] = outs[at].reshape(part)
    return tuple(outs)


def solution(mesh):
    rows, vector, grid = P("fsdp", None), P("fsdp"), P("fsdp", "seq", None, None)
    return jax.shard_map(
        shards,
        mesh=mesh,
        in_specs=(grid, grid, P(), P(), vector, vector, rows, rows, rows, vector, vector, rows, rows),
        out_specs=(grid, grid, vector, vector, rows, rows, rows, vector, vector, rows, rows),
        check_vma=False,
    )
```

```python
import functools

import jax
import jax.numpy as jnp
from jax import lax
from jax.experimental import pallas as pl
from jax.experimental.pallas import tpu as pltpu
from jax.sharding import PartitionSpec as P

WS = 7
SHIFT = 3
SLOT = 64
LANES = 256
SPREAD = 2
CUTS = 1

EPSILON = 1e-05
MASKED = -100.0
REMOVED = -1e30
SQRT_HALF = 0.7071067811865476
INV_ROOT_TAU = 0.3989422804014327

F32 = jnp.float32
LOW = jnp.bfloat16


def dot(left, right, left_dim, right_dim):
    dims = (((left_dim,), (right_dim,)), ((), ()))
    return lax.dot_general(left, right, dims, preferred_element_type=F32)


def nn(left, right):
    return dot(left, right, 1, 0)


def nt(left, right):
    return dot(left, right, 1, 1)


def tn(left, right):
    return dot(left, right, 0, 0)


def iota(shape, dim):
    return lax.broadcasted_iota(jnp.int32, shape, dim)


def split(values):
    high = values.astype(LOW)
    return high, (values - high.astype(F32)).astype(LOW)


def sum_exact(values, ones):
    high, low = split(values)
    both = nn(jnp.concatenate([high, low], axis=0), ones)
    return both[: values.shape[0]] + both[values.shape[0] :]


def layer_norm(values, norm_gain, norm_offset):
    average = jnp.mean(values, axis=-1, keepdims=True)
    centred = values - average
    variance = jnp.mean(centred * centred, axis=-1, keepdims=True)
    inverse = lax.rsqrt(variance + EPSILON)
    normed = centred * inverse
    return normed * norm_gain + norm_offset, normed, inverse


def norm_back(upstream, normed, inverse, norm_gain):
    scaled = upstream * norm_gain
    mean_grad = jnp.mean(scaled, axis=-1, keepdims=True)
    second = jnp.mean(scaled * normed, axis=-1, keepdims=True)
    grad_in = inverse * (scaled - mean_grad - normed * second)
    gain_grad = jnp.sum(upstream * normed, axis=0, keepdims=True)
    return grad_in, gain_grad, jnp.sum(upstream, axis=0, keepdims=True)


def gelu_parts(hidden):
    normal_cdf = 0.5 * (1.0 + lax.erf(hidden * SQRT_HALF))
    density = jnp.exp(-0.5 * hidden * hidden) * INV_ROOT_TAU
    return hidden * normal_cdf, normal_cdf + hidden * density


def divide(values, by):
    if by & (by - 1):
        return values // by
    return lax.shift_right_logical(values, jnp.int32(by.bit_length() - 1))


def place_of(slot_at, num_cols):
    window = divide(slot_at, SLOT)
    spot = slot_at - window * SLOT
    across = num_cols // WS
    row_in = sum((spot >= WS * step).astype(jnp.int32) for step in range(1, WS))
    band = divide(window, across)
    row = band * WS + row_in
    col = (window - band * across) * WS + spot - row_in * WS
    return row, col, spot < WS * WS


class Dims:
    def __init__(self, owners, size, num_rows, num_cols, width, hidden, num_heads, entries):
        self.owners, self.size = owners, size
        self.pairs, self.halves = owners // 2, size // 2
        self.num_rows, self.num_cols, self.width = num_rows, num_cols, width
        self.hidden, self.num_heads, self.entries = hidden, num_heads, entries
        self.windows = (num_rows // WS) * (num_cols // WS)
        self.slots = self.windows * SLOT
        self.stride = -(-num_cols // 16) * 16
        self.natural = -(-num_rows * self.stride // 128) * 128
        self.part = width // owners
        self.scatter = self.part % (16 * size) == 0
        self.fine = self.halves if self.scatter else 1
        self.piece = self.part // (2 * self.fine)
        self.tiles = hidden // width
        self.groups = width // LANES
        self.per_group = num_heads // self.groups
        self.head_dim = width // num_heads
        self.chunks = (2 * self.tiles + 4) * CUTS
        self.cut = width // CUTS
        pairs, halves = self.pairs, self.halves
        self.copies = 64 + 9 * (3 * pairs - 2) + self.chunks * (pairs + 1 + 2 * (halves - 1))
        self.copies += pairs + size


def body(d, *refs):
    (tok, cot, reg, rel, gain_a, offset_a, gain_b, offset_b, table) = refs[:9]
    weights = refs[9:13]
    (out, tok_grad, d_gain_a, d_offset_a, d_table, d_gain_b, d_offset_b, result) = refs[13:21]
    fulls = refs[21:25]
    (small, halo_tok, halo_cot, halo_out, halo_grad, came_grad, natural, hat_a, hat_b, middle, low_a) = refs[25:36]
    (qkv, probs, attended, slope, act, perm, perm_t, heads, ones, onehot, rel_pad, bias, spread, mask) = refs[36:50]
    (at_a, at_a_in, at_b, at_b_in, at_c, at_c_in, at_d, at_d_in, g_cot, g_hid, g_mid, g_qkv) = refs[50:62]
    (grads, in_two, sum_two, in_three, sum_three, in_four, small_grad, small_in, small_sum, small_two, small_all, table_sum) = refs[62:74]
    send_sem, recv_sem, copy_sem = refs[74:]

    pairs, halves, size, owners = d.pairs, d.halves, d.size, d.owners
    width, part = d.width, d.part
    place, line = lax.axis_index("fsdp"), lax.axis_index("seq")
    pair, core = place // 2, place % 2
    half, side = line // 2, line % 2
    mesh_id = pl.DeviceIdType.MESH
    partner = {"fsdp": pair * 2 + 1 - core, "seq": line}
    beside = {"fsdp": place, "seq": half * 2 + 1 - side}
    pair_peers = [(pair + step) % pairs for step in range(1, pairs)]
    pair_sources = [(pair + pairs - step) % pairs for step in range(1, pairs)]
    across = [{"fsdp": peer * 2 + core, "seq": line} for peer in pair_peers]
    half_peers = [(half + step) % halves for step in range(1, halves)]
    along = [{"fsdp": place, "seq": peer * 2 + side} for peer in half_peers]
    seq_peers = [{"fsdp": place, "seq": (line + step) % size} for step in range(1, size)]
    later, earlier = seq_peers[0], seq_peers[-1]

    used = [0]
    started = []

    def send(source, target, device):
        slot = used[0]
        used[0] += 1
        copy = pltpu.make_async_remote_copy(
            src_ref=source,
            dst_ref=target,
            send_sem=send_sem.at[slot],
            recv_sem=recv_sem.at[slot],
            device_id=device,
            device_id_type=mesh_id,
        )
        copy.start()
        started.append(copy)
        return copy

    small[place] = jnp.zeros(small.shape[1:], F32)
    for at, vector in enumerate((gain_a, offset_a, gain_b, offset_b)):
        small[place, at : at + 1, :part] = vector[...].astype(F32)
    table_rows = table.shape[0]
    small[place, 4 : 4 + table_rows, : d.entries] = table[...].astype(F32)

    barrier = pltpu.get_barrier_semaphore()
    greeted = [partner] + across + seq_peers
    for device in greeted:
        pl.semaphore_signal(barrier, inc=1, device_id=device, device_id_type=mesh_id)
    pl.semaphore_wait(barrier, len(greeted))

    pieces = []
    for at, count in enumerate((3, 1, 2, 2)):
        rows, columns = weights[at].shape[1:]
        for step in range(count):
            if columns // count % 128:
                where = (pl.ds(step * (rows // count), rows // count), slice(None))
            else:
                where = (slice(None), pl.ds(step * (columns // count), columns // count))
            pieces.append((at,) + where)
    far, near, home, kept = {}, {}, {}, {}

    def gather_far(index):
        at, rows, columns = pieces[index]
        for step, device in enumerate(across):
            source = weights[at].at[side, rows, columns]
            far[index, step] = send(source, fulls[at].at[place, side, rows, columns], device)

    def gather_near(index):
        at, rows, columns = pieces[index]
        for step, source in enumerate(pair_sources):
            far[index, step].wait_recv()
            came = fulls[at].at[source * 2 + core, side, rows, columns]
            near[index, step] = send(came, came, beside)
        if index + window_far < len(pieces):
            gather_far(index + window_far)

    def gather_home(index):
        at, rows, columns = pieces[index]
        for step, source in enumerate(pair_sources):
            near[index, step].wait_recv()
            came = fulls[at].at[source * 2 + core, :, rows, columns]
            home.setdefault(at, []).append(send(came, came, partner))

    window_far = 4
    gathers = sorted(
        (index + lag, lag, index) for index in range(len(pieces)) for lag in range(2)
    )

    def gather(count):
        for _ in range(min(count, len(gathers))):
            _, lag, index = gathers.pop(0)
            (gather_home if lag else gather_near)(index)

    def gather_done(at):
        last_piece = max(index for index, piece in enumerate(pieces) if piece[0] == at)
        while any(lag == 1 and index <= last_piece for _, lag, index in gathers):
            gather(1)
        for copy in home[at]:
            copy.wait_recv()
        kept[at].wait()

    own_small = small.at[place]
    small_far = [send(own_small, own_small, device) for device in across]
    small_home = [send(own_small, own_small, partner)]
    for index in range(window_far):
        gather_far(index)
    halo_copies = [send(tok.at[0, 0:SHIFT], halo_tok, earlier)]
    halo_copies.append(send(cot.at[0, 0:SHIFT], halo_cot, earlier))
    for at in range(len(weights)):
        home[at] = [send(weights[at], fulls[at].at[place], partner)]
        kept[at] = pltpu.make_async_copy(weights[at], fulls[at].at[place], copy_sem.at[at])
        kept[at].start()

    def token_of(slot_at):
        row, col, real = place_of(slot_at, d.num_cols)
        token_col = jnp.where(col + SHIFT >= d.num_cols, col + SHIFT - d.num_cols, col + SHIFT)
        return jnp.where(real, row * d.stride + token_col, -1)

    hit = iota((d.slots, d.natural), 1) == token_of(iota((d.slots, 1), 0))
    perm[...] = jnp.where(hit, 1.0, 0.0).astype(LOW)
    hit = iota((d.natural, d.slots), 0) == token_of(iota((1, d.slots), 1))
    perm_t[...] = jnp.where(hit, 1.0, 0.0).astype(LOW)
    span = d.per_group * SLOT
    block_down = divide(iota((span, 1), 0), SLOT)
    hit = block_down == divide(iota((1, LANES), 1), d.head_dim)
    heads[...] = jnp.where(hit, 1.0, 0.0).astype(LOW)
    hit = block_down == divide(iota((1, span), 1), SLOT)
    ones[...] = jnp.where(hit, 1.0, 0.0).astype(LOW)

    grid_cols, grid_rows = reg.shape
    row, col, real = place_of(iota((d.slots, 1), 0), d.num_cols)
    picked = jnp.where(iota((d.slots, grid_rows), 1) == line * d.num_rows + row, 1.0, 0.0)
    by_row = nt(picked.astype(LOW), reg[...].astype(F32).astype(LOW))
    regions = jnp.sum(
        jnp.where(iota((d.slots, grid_cols), 1) == col, by_row, 0.0), axis=1, keepdims=True
    )
    regions_t = jnp.transpose(jnp.broadcast_to(regions, (d.slots, 128)))
    for window in range(d.windows):
        down = regions[window * SLOT : (window + 1) * SLOT]
        over = regions_t[0:1, window * SLOT : (window + 1) * SLOT]
        added = jnp.where(down == over, 0.0, MASKED).astype(F32)
        mask[window] = jnp.concatenate([added, added], axis=1)

    positions = rel.shape[0]
    rel_pad[...] = jnp.full(rel_pad.shape, -1.0, F32)
    rel_pad[:positions, :positions] = rel[...].astype(F32)
    rel_pad[...] = jnp.transpose(rel_pad[...])
    table_lanes = small.shape[2]

    rel_t = rel_pad[:SLOT]
    for at in range(onehot.shape[0]):
        hit = rel_t[:, at : at + 1] == iota((1, table_lanes), 1).astype(F32)
        onehot[at] = jnp.where(hit, 1.0, 0.0).astype(LOW)

    natural[...] = jnp.zeros(natural.shape, LOW)
    keep = d.num_rows - SHIFT

    def windowed(field, halo, copy):
        copy.wait_recv()
        for at in range(d.num_rows):
            source = field[0, at + SHIFT] if at < keep else halo[at - keep]
            natural[at * d.stride : at * d.stride + d.num_cols] = source
        return nn(perm[...], natural[...])

    inputs = windowed(tok, halo_tok, halo_copies[0])

    for step, source in enumerate(pair_sources):
        small_far[step].wait_recv()
        came = small.at[source * 2 + core]
        small_home.append(send(came, came, partner))
    for copy in small_home:
        copy.wait_recv()

    def vector_of(at):
        return jnp.concatenate([small[owner, at : at + 1, :part] for owner in range(owners)], axis=1)

    norm_gain_a, norm_offset_a, norm_gain_b, norm_offset_b = [vector_of(at) for at in range(4)]
    normed, normed_hat, inverse_a = layer_norm(inputs, norm_gain_a, norm_offset_a)
    hat_a[...] = normed_hat
    low_a[...] = normed.astype(LOW)

    def by_owner(values):
        rows = values.shape[0] // owners
        return values.reshape(pairs, 2, rows, values.shape[1])

    at_a[...] = by_owner(jnp.transpose(low_a[...]))
    swaps = {}
    swaps["a"] = send(at_a.at[:, 1 - core], at_a_in, partner)
    gather(2)

    whole_table = jnp.concatenate(
        [small[owner, 4 : 4 + table_rows] for owner in range(owners)], axis=0
    ).astype(LOW)

    batch = LANES // SLOT
    for step in range(onehot.shape[0] // batch):
        picks = onehot[step * batch : (step + 1) * batch].reshape(batch * SLOT, table_lanes)
        found = nt(whole_table, picks)
        for at in range(batch):
            spread[pl.ds(step * batch + at, d.num_heads, stride=SLOT), :SLOT] = found[:, at * SLOT : (at + 1) * SLOT]

    removed = jnp.where(iota((SLOT, SLOT), 1) < WS * WS, 0.0, REMOVED)
    for head in range(0, d.num_heads, 2):
        one = spread[head * SLOT : (head + 1) * SLOT, :SLOT] + removed
        two = spread[(head + 1) * SLOT : (head + 2) * SLOT, :SLOT] + removed
        bias[:, head * SLOT : (head + 2) * SLOT] = jnp.concatenate([one, two], axis=1)

    gather(1)
    g_cot[0] = windowed(cot, halo_cot, halo_copies[1]).astype(LOW)
    swaps["cot"] = send(g_cot.at[0], g_cot.at[1], partner)
    gather_done(0)

    def weight(at, cols):
        values = fulls[at][:, :, :, cols]
        return values.reshape(-1, values.shape[-1])

    scale = d.head_dim ** (-0.5)
    for at in range(3):
        columns = pl.ds(at * width, width)
        values = nn(low_a[...], weight(0, columns))
        qkv[at] = (values * scale if at == 0 else values).astype(LOW)

    def span_of(window, group):
        return pl.ds(window * SLOT, SLOT), pl.ds(group * LANES, LANES)

    def blocks_of(tile):
        return jnp.concatenate([tile] * d.per_group, axis=0) * heads[...]

    for window in range(d.windows):
        for group in range(d.groups):
            rows, lanes = span_of(window, group)
            scores = nt(qkv[0, rows, lanes], blocks_of(qkv[1, rows, lanes]))
            scores += bias[:, group * span : (group + 1) * span]
            scores += jnp.concatenate([mask[window]] * (d.per_group // 2), axis=1)
            powers = jnp.exp(scores)
            share = powers / sum_exact(powers, ones[...])
            probs[window, group] = share
            found = nn(share.astype(LOW), blocks_of(qkv[2, rows, lanes]))
            attended[rows, lanes] = found.astype(LOW)
        gather(1)
    at_c[...] = by_owner(jnp.transpose(attended[...]))
    swaps["c"] = send(at_c.at[:, 1 - core], at_c_in, partner)
    gather_done(1)
    middle[...] = inputs + nn(attended[...], weight(1, slice(None)))
    normed, normed_hat, inverse_b = layer_norm(middle[...], norm_gain_b, norm_offset_b)
    hat_b[...] = normed_hat
    low_b = normed.astype(LOW)
    at_b[...] = by_owner(jnp.transpose(low_b))
    swaps["b"] = send(at_b.at[:, 1 - core], at_b_in, partner)
    gather_done(2)

    tile_owners = owners // d.tiles
    for tile in range(d.tiles):
        columns = pl.ds(tile * width, width)
        hidden = nn(low_b, weight(2, columns))
        activated, slope_tile = gelu_parts(hidden)
        slope[tile] = slope_tile
        act_low = activated.astype(LOW)
        act[:, tile * width : (tile + 1) * width] = act_low
        turned = jnp.transpose(act_low).reshape(tile_owners, -1, d.slots)
        for at in range(tile_owners):
            owner = tile * tile_owners + at
            at_d[owner // 2, owner % 2] = turned[at]
            if owner % 2:
                pair_at = owner // 2
                copy = send(at_d.at[pair_at, 1 - core], at_d_in.at[pair_at], partner)
                swaps["d", pair_at] = copy

    stage_copies = {}

    def reduce_start(block, own, came, right, came_right):
        own, came = own.reshape(-1, d.slots), came.reshape(-1, d.slots)
        for step in range(CUTS):
            chunk, columns = block * CUTS + step, slice(step * d.cut, (step + 1) * d.cut)
            total = nn(own, right[:, columns]) + nn(came, came_right[:, columns])
            grads[chunk] = total.astype(LOW).reshape(grads.shape[1:])
            stage_copies[chunk, 0] = [
                send(grads.at[chunk, peer], in_two.at[chunk, at], device)
                for at, (peer, device) in enumerate(zip(pair_peers, across))
            ]

    def wide(ref, *index):
        return ref[index].astype(F32)

    def stage_two(chunk):
        total = wide(grads, chunk, pair)
        for step in range(pairs - 1):
            total += wide(in_two, chunk, step)
        sum_two[chunk] = total.astype(LOW)
        return [send(sum_two.at[chunk, 1 - side], in_three.at[chunk], beside)]

    def stage_three(chunk):
        total = (wide(sum_two, chunk, side) + wide(in_three, chunk)).astype(LOW)
        sum_three[chunk] = total
        if d.scatter:
            return [
                send(sum_three.at[chunk, peer], in_four.at[chunk, step], device)
                for step, (peer, device) in enumerate(zip(half_peers, along))
            ]
        in_four[chunk, half] = total[0]
        mine = in_four.at[chunk, half]
        return [send(sum_three.at[chunk, 0], mine, device) for device in along]

    def stage_four(chunk):
        if d.scatter:
            total = wide(sum_three, chunk, half)
            for step in range(halves - 1):
                total += wide(in_four, chunk, step)
            result[chunk, side, half] = total.astype(LOW)
            mine = result.at[chunk, side, half]
            return [send(mine, mine, device) for device in along]
        total = wide(in_four, chunk, 0)
        for at in range(1, halves):
            total += wide(in_four, chunk, at)
        result[chunk, side, 0] = total.astype(LOW)
        return []

    def stage_five(chunk):
        mine = result.at[chunk, side]
        return [send(mine, mine, beside)]

    def stage_six(chunk):
        return []

    stages = (stage_two, stage_three, stage_four, stage_five, stage_six)
    events = sorted(
        (chunk + SPREAD * lag, lag, chunk) for chunk in range(d.chunks) for lag in range(len(stages))
    )

    def advance(limit):
        while events and events[0][0] <= limit:
            _, lag, chunk = events.pop(0)
            for copy in stage_copies[chunk, lag]:
                copy.wait_recv()
            stage_copies[chunk, lag + 1] = stages[lag](chunk)

    swaps["cot"].wait_recv()
    for pair_at in range(pairs):
        swaps["d", pair_at].wait_recv()
    for chunk in range(d.tiles):
        rows = pl.ds(chunk * part, part)
        reduce_start(chunk, at_d[:, core, rows], at_d_in[:, rows], g_cot[0], g_cot[1])

    gather_done(3)
    for tile in range(d.tiles):
        whole = fulls[3][tile * tile_owners : (tile + 1) * tile_owners].reshape(width, width)
        hidden_grad = (nt(g_cot[0], whole) * slope[tile]).astype(LOW)
        g_hid[tile, 0] = hidden_grad
        swaps["h", tile] = send(g_hid.at[tile, 0], g_hid.at[tile, 1], partner)
        term = nt(hidden_grad, weight(2, pl.ds(tile * width, width)))
        upstream_two = term if tile == 0 else upstream_two + term
    swaps["b"].wait_recv()
    for tile in range(d.tiles):
        swaps["h", tile].wait_recv()
        reduce_start(d.tiles + tile, at_b[:, core], at_b_in[...], g_hid[tile, 0], g_hid[tile, 1])

    out_tiles = (middle[...] + nn(act[...], fulls[3][...].reshape(-1, width))).astype(LOW)
    out_rows = nn(perm_t[...], out_tiles).astype(LOW)
    for at in range(d.num_rows):
        field = out_rows[at * d.stride : at * d.stride + d.num_cols]
        if at < keep:
            out[0, at + SHIFT] = field
        else:
            halo_out[at - keep] = field
    last = [send(halo_out, out.at[0, 0:SHIFT], later)]

    advance(1)
    back_two, gain_b_grad, offset_b_grad = norm_back(upstream_two, hat_b[...], inverse_b, norm_gain_b)
    middle_grad = g_cot[0].astype(F32) + back_two
    middle_low = middle_grad.astype(LOW)
    g_mid[0] = middle_low
    swaps["m"] = send(g_mid.at[0], g_mid.at[1], partner)
    attended[...] = nt(middle_low, weight(1, slice(None))).astype(LOW)
    middle[...] = middle_grad
    swaps["m"].wait_recv()
    swaps["c"].wait_recv()
    reduce_start(2 * d.tiles, at_c[:, core], at_c_in[...], g_mid[0], g_mid[1])
    advance(2)

    def fold(values):
        kept_lanes = values * heads[...].astype(F32)
        return jnp.sum(kept_lanes.reshape(d.per_group, SLOT, LANES), axis=0)

    for window in range(d.windows):
        for group in range(d.groups):
            rows, lanes = span_of(window, group)
            query, key, value = [qkv[at, rows, lanes] for at in range(3)]
            keys = blocks_of(key)
            share = probs[window, group]
            given = attended[rows, lanes]
            prob_grad = nt(given, blocks_of(value))
            inner = sum_exact(share * prob_grad, ones[...])
            score_grad = share * (prob_grad - inner)
            score_low = score_grad.astype(LOW)
            across_heads = slice(group * span, (group + 1) * span)
            if window == 0:
                bias[:, across_heads] = score_grad
            else:
                bias[:, across_heads] += score_grad
            g_qkv[0, 0, rows, lanes] = (nn(score_low, keys) * scale).astype(LOW)
            g_qkv[1, 0, rows, lanes] = fold(tn(score_low, query)).astype(LOW)
            g_qkv[2, 0, rows, lanes] = fold(tn(share.astype(LOW), given)).astype(LOW)
        advance(3 + window)

    for at in range(3):
        swaps["q", at] = send(g_qkv.at[at, 0], g_qkv.at[at, 1], partner)
    swaps["a"].wait_recv()
    for at in range(3):
        term = nt(g_qkv[at, 0], weight(0, pl.ds(at * width, width)))
        upstream_one = term if at == 0 else upstream_one + term
        swaps["q", at].wait_recv()
        reduce_start(2 * d.tiles + 1 + at, at_a[:, core], at_a_in[...], g_qkv[at, 0], g_qkv[at, 1])
    advance(7)

    back_one, gain_a_grad, offset_a_grad = norm_back(upstream_one, hat_a[...], inverse_a, norm_gain_a)

    for head in range(d.num_heads):
        spread[head * SLOT : (head + 1) * SLOT, :SLOT] = bias[:, head * SLOT : (head + 1) * SLOT]

    for step in range(onehot.shape[0] // batch):
        pieces = [
            spread[pl.ds(step * batch + at, d.num_heads, stride=SLOT), :SLOT] for at in range(batch)
        ]
        high, low = split(jnp.concatenate(pieces, axis=1))
        picks = onehot[pl.ds(step * batch, batch)].reshape(batch * SLOT, table_lanes)
        table_sum[step] = nn(jnp.concatenate([high, low], axis=0), picks)

    table_total = jnp.sum(table_sum[...], axis=0)
    table_grad = table_total[: d.num_heads] + table_total[d.num_heads :]
    small_grad[...] = jnp.zeros(small_grad.shape, F32)
    vector_grads = (gain_a_grad, offset_a_grad, gain_b_grad, offset_b_grad)
    for owner in range(owners):
        spot = (owner // 2, owner % 2)
        for at, vector in enumerate(vector_grads):
            small_grad[spot + (slice(at, at + 1), slice(0, part))] = vector[:, owner * part : (owner + 1) * part]
        rows = table_grad[owner * table_rows : (owner + 1) * table_rows]
        small_grad[spot + (slice(4, 4 + table_rows),)] = rows
    small_home = send(small_grad.at[:, 1 - core], small_in, partner)
    advance(8)

    final = middle[...] + back_one
    high, low = split(final)
    final_rows = nn(perm_t[...], high) + nn(perm_t[...], low)
    for at in range(d.num_rows):
        field = final_rows[at * d.stride : at * d.stride + d.num_cols]
        if at < keep:
            tok_grad[0, at + SHIFT] = field
        else:
            halo_grad[at - keep] = field.astype(LOW)
    grad_copy = send(halo_grad, came_grad, later)

    small_home.wait_recv()
    small_sum[...] = small_grad[:, core] + small_in[...]
    small_far = [
        send(small_sum.at[peer], small_two.at[step], device)
        for step, (peer, device) in enumerate(zip(pair_peers, across))
    ]
    advance(9)
    total = small_sum[pair]
    for step in range(pairs - 1):
        small_far[step].wait_recv()
        total += small_two[step]
    small_all[line] = total
    mine = small_all.at[line]
    small_copies = [send(mine, mine, device) for device in seq_peers]
    advance(d.chunks + 2)
    grad_copy.wait_recv()
    for at in range(SHIFT):
        tok_grad[0, at] = came_grad[at].astype(F32)
    for copy in small_copies:
        copy.wait_recv()
    total = small_all[0]
    for at in range(1, size):
        total += small_all[at]
    for at, target in enumerate((d_gain_a, d_offset_a, d_gain_b, d_offset_b)):
        target[...] = total[at : at + 1, :part]
    d_table[...] = total[4 : 4 + table_rows, : d.entries]
    advance(d.chunks + SPREAD * len(stages))

    for copy in last:
        copy.wait_recv()
    for copy in started:
        copy.wait_send()


def pass_on(d, *refs):
    sources, targets = refs[:8], refs[8:]
    for at, (source, target) in enumerate(zip(sources[:7], targets[:7])):
        target[...] = source[0].reshape(target.shape) if at == 1 else source[...]
    totals, (qkv, proj, expand, reduce) = sources[7], targets[7:]
    for chunk in range(d.chunks):
        total = totals[chunk].astype(F32).reshape(d.part, d.cut)
        block, step = chunk // CUTS, chunk % CUTS
        if block < d.tiles:
            reduce[block * d.part : (block + 1) * d.part, step * d.cut : (step + 1) * d.cut] = total
            continue
        if block < 2 * d.tiles:
            target, start = expand, chunk - d.tiles * CUTS
        elif block == 2 * d.tiles:
            target, start = proj, step
        else:
            target, start = qkv, chunk - (2 * d.tiles + 1) * CUTS
        target[:, start * d.cut : (start + 1) * d.cut] = total


def shards(
    tokens,
    cotangent,
    region_ids,
    relative_index,
    first_gain,
    first_offset,
    qkv_weight,
    proj_weight,
    bias_table,
    second_gain,
    second_offset,
    expand_weight,
    reduce_weight,
):
    owners = lax.axis_size("fsdp")
    size = lax.axis_size("seq")
    _, num_rows, num_cols, width = tokens.shape
    table_rows, entries = bias_table.shape
    hidden = expand_weight.shape[1]
    num_heads = table_rows * owners
    d = Dims(owners, size, num_rows, num_cols, width, hidden, num_heads, entries)
    pairs, halves, part = d.pairs, d.halves, d.part
    slots, span = d.slots, d.per_group * SLOT
    weights = [
        weight.reshape(2, weight.shape[0] // 2, weight.shape[1])
        for weight in (qkv_weight, proj_weight, expand_weight, reduce_weight)
    ]
    vectors = [
        vector.reshape(1, part) for vector in (first_gain, first_offset, second_gain, second_offset)
    ]
    entry_lanes = -(-entries // 128) * 128
    small_rows = -(-(4 + table_rows) // 8) * 8
    held = -(-WS * WS // 4) * 4
    chunks, fine, piece = d.chunks, d.fine, d.piece
    hidden_part = hidden // owners

    def low(*shape):
        return pltpu.VMEM(shape, LOW)

    def full(*shape):
        return pltpu.VMEM(shape, F32)

    scratch = [low(owners, *weight.shape) for weight in weights]
    scratch += [
        full(owners, small_rows, entry_lanes),
        low(SHIFT, num_cols, width),
        low(SHIFT, num_cols, width),
        low(SHIFT, num_cols, width),
        low(SHIFT, num_cols, width),
        low(SHIFT, num_cols, width),
        low(d.natural, width),
        full(slots, width),
        full(slots, width),
        full(slots, width),
        low(slots, width),
    ]
    scratch += [
        low(3, slots, width),
        full(d.windows, d.groups, SLOT, span),
        low(slots, width),
        full(d.tiles, slots, width),
        low(slots, hidden),
        low(slots, d.natural),
        low(d.natural, slots),
        low(span, LANES),
        low(span, span),
        low(held, SLOT, entry_lanes),
        full(128, 128),
        full(SLOT, num_heads * SLOT),
        full(num_heads * SLOT, 128),
        full(d.windows, SLOT, 2 * SLOT),
    ]
    for rows in (part, part, part, hidden_part):
        scratch += [low(pairs, 2, rows, slots), low(pairs, rows, slots)]
    scratch += [
        low(2, slots, width),
        low(d.tiles, 2, slots, width),
        low(2, slots, width),
        low(3, 2, slots, width),
    ]
    scratch += [
        low(chunks, pairs, 2, fine, piece, d.cut),
        low(chunks, max(pairs - 1, 1), 2, fine, piece, d.cut),
        low(chunks, 2, fine, piece, d.cut),
        low(chunks, fine, piece, d.cut),
        low(chunks, fine, piece, d.cut),
        low(chunks, halves, piece, d.cut),
        full(pairs, 2, small_rows, entry_lanes),
        full(pairs, small_rows, entry_lanes),
        full(pairs, small_rows, entry_lanes),
        full(max(pairs - 1, 1), small_rows, entry_lanes),
        full(size, small_rows, entry_lanes),
        full(held * SLOT // LANES, 2 * num_heads, entry_lanes),
    ]
    scratch += [pltpu.SemaphoreType.DMA((d.copies,))] * 2
    scratch += [pltpu.SemaphoreType.DMA((len(weights),))]

    def shape(*dims):
        return jax.ShapeDtypeStruct(dims, F32)

    in_vmem = pl.BlockSpec(memory_space=pltpu.VMEM)
    outs = pl.pallas_call(
        functools.partial(body, d),
        out_shape=[
            jax.ShapeDtypeStruct(tokens.shape, LOW),
            shape(*tokens.shape),
            shape(1, part),
            shape(1, part),
            shape(table_rows, entries),
            shape(1, part),
            shape(1, part),
            jax.ShapeDtypeStruct((chunks, 2, fine, piece, d.cut), LOW),
        ],
        in_specs=[in_vmem] * 13,
        out_specs=[in_vmem] * 8,
        scratch_shapes=scratch,
        compiler_params=pltpu.CompilerParams(
            collective_id=0, has_side_effects=True, vmem_limit_bytes=60 * 1024 * 1024
        ),
    )(tokens, cotangent, region_ids.T, relative_index, *vectors, bias_table, *weights)
    shapes = [jax.ShapeDtypeStruct(o.shape, o.dtype) for o in outs[:-1]]
    shapes[1] = shape(num_rows, num_cols, 1, width)
    shapes += [shape(part, 3 * width), shape(part, width), shape(part, hidden), shape(hidden_part, width)]
    outs = pl.pallas_call(
        functools.partial(pass_on, d),
        out_shape=shapes,
        in_specs=[in_vmem] * 8,
        out_specs=[in_vmem] * len(shapes),
        compiler_params=pltpu.CompilerParams(vmem_limit_bytes=60 * 1024 * 1024),
    )(*outs)
    out, tok_grad, gain_a, offset_a, table_grad, gain_b, offset_b, qkv, proj, expand, reduce = outs
    gain_a, offset_a, gain_b, offset_b = [o.reshape(part) for o in (gain_a, offset_a, gain_b, offset_b)]
    tok_grad = tok_grad.reshape(tokens.shape)
    return out, tok_grad, gain_a, offset_a, qkv, proj, table_grad, gain_b, offset_b, expand, reduce


def solution(mesh):
    rows, vector, grid = P("fsdp", None), P("fsdp"), P("fsdp", "seq", None, None)
    return jax.shard_map(
        shards,
        mesh=mesh,
        in_specs=(grid, grid, P(), P(), vector, vector, rows, rows, rows, vector, vector, rows, rows),
        out_specs=(grid, grid, vector, vector, rows, rows, rows, vector, vector, rows, rows),
        check_vma=False,
    )
```

```python
import functools

import jax
import jax.numpy as jnp
from jax import lax
from jax.experimental import pallas as pl
from jax.experimental.pallas import tpu as pltpu
from jax.sharding import PartitionSpec as P

WS = 7
SHIFT = 3
SLOT = 64
LANES = 256
SPREAD = 2
CUTS = 1

EPSILON = 1e-05
MASKED = -100.0
REMOVED = -1e30
SQRT_HALF = 0.7071067811865476
INV_ROOT_TAU = 0.3989422804014327

F32 = jnp.float32
LOW = jnp.bfloat16


def dot(left, right, left_dim, right_dim):
    dims = (((left_dim,), (right_dim,)), ((), ()))
    return lax.dot_general(left, right, dims, preferred_element_type=F32)


def nn(left, right):
    return dot(left, right, 1, 0)


def nt(left, right):
    return dot(left, right, 1, 1)


def tn(left, right):
    return dot(left, right, 0, 0)


def iota(shape, dim):
    return lax.broadcasted_iota(jnp.int32, shape, dim)


def split(values):
    high = values.astype(LOW)
    return high, (values - high.astype(F32)).astype(LOW)


def sum_exact(values, ones):
    high, low = split(values)
    both = nn(jnp.concatenate([high, low], axis=0), ones)
    return both[: values.shape[0]] + both[values.shape[0] :]


def layer_norm(values, norm_gain, norm_offset):
    average = jnp.mean(values, axis=-1, keepdims=True)
    centred = values - average
    variance = jnp.mean(centred * centred, axis=-1, keepdims=True)
    inverse = lax.rsqrt(variance + EPSILON)
    normed = centred * inverse
    return normed * norm_gain + norm_offset, normed, inverse


def norm_back(upstream, normed, inverse, norm_gain):
    scaled = upstream * norm_gain
    mean_grad = jnp.mean(scaled, axis=-1, keepdims=True)
    second = jnp.mean(scaled * normed, axis=-1, keepdims=True)
    grad_in = inverse * (scaled - mean_grad - normed * second)
    gain_grad = jnp.sum(upstream * normed, axis=0, keepdims=True)
    return grad_in, gain_grad, jnp.sum(upstream, axis=0, keepdims=True)


def gelu_parts(hidden):
    normal_cdf = 0.5 * (1.0 + lax.erf(hidden * SQRT_HALF))
    density = jnp.exp(-0.5 * hidden * hidden) * INV_ROOT_TAU
    return hidden * normal_cdf, normal_cdf + hidden * density


def divide(values, by):
    if by & (by - 1):
        return values // by
    return lax.shift_right_logical(values, jnp.int32(by.bit_length() - 1))


def place_of(slot_at, num_cols):
    window = divide(slot_at, SLOT)
    spot = slot_at - window * SLOT
    across = num_cols // WS
    row_in = sum((spot >= WS * step).astype(jnp.int32) for step in range(1, WS))
    band = divide(window, across)
    row = band * WS + row_in
    col = (window - band * across) * WS + spot - row_in * WS
    return row, col, spot < WS * WS


class Dims:
    def __init__(self, owners, size, num_rows, num_cols, width, hidden, num_heads, entries):
        self.owners, self.size = owners, size
        self.pairs, self.halves = owners // 2, size // 2
        self.num_rows, self.num_cols, self.width = num_rows, num_cols, width
        self.hidden, self.num_heads, self.entries = hidden, num_heads, entries
        self.windows = (num_rows // WS) * (num_cols // WS)
        self.slots = self.windows * SLOT
        self.stride = -(-num_cols // 16) * 16
        self.natural = -(-num_rows * self.stride // 128) * 128
        self.part = width // owners
        self.scatter = self.part % (16 * size) == 0
        self.fine = self.halves if self.scatter else 1
        self.piece = self.part // (2 * self.fine)
        self.tiles = hidden // width
        self.groups = width // LANES
        self.per_group = num_heads // self.groups
        self.head_dim = width // num_heads
        self.chunks = (2 * self.tiles + 4) * CUTS
        self.cut = width // CUTS
        pairs, halves = self.pairs, self.halves
        self.copies = 64 + 9 * (3 * pairs - 2) + self.chunks * (pairs + 1 + 2 * (halves - 1))
        self.copies += pairs + size


def body(d, *refs):
    (tok, cot, reg, rel, gain_a, offset_a, gain_b, offset_b, table) = refs[:9]
    weights = refs[9:13]
    (out, tok_grad, d_gain_a, d_offset_a, d_table, d_gain_b, d_offset_b, result) = refs[13:21]
    fulls = refs[21:25]
    (small, halo_tok, halo_cot, halo_out, halo_grad, came_grad, natural, hat_a, hat_b, middle, low_a) = refs[25:36]
    (qkv, probs, attended, slope, act, perm, perm_t, heads, ones, onehot, rel_pad, bias, spread, mask) = refs[36:50]
    (at_a, at_a_in, at_b, at_b_in, at_c, at_c_in, at_d, at_d_in, g_cot, g_hid, g_mid, g_qkv) = refs[50:62]
    (grads, in_two, sum_two, in_three, sum_three, in_four, small_grad, small_in, small_sum, small_two, small_all, table_sum) = refs[62:74]
    send_sem, recv_sem, copy_sem = refs[74:]

    pairs, halves, size, owners = d.pairs, d.halves, d.size, d.owners
    width, part = d.width, d.part
    place, line = lax.axis_index("fsdp"), lax.axis_index("seq")
    pair, core = place // 2, place % 2
    half, side = line // 2, line % 2
    mesh_id = pl.DeviceIdType.MESH
    partner = {"fsdp": pair * 2 + 1 - core, "seq": line}
    beside = {"fsdp": place, "seq": half * 2 + 1 - side}
    pair_peers = [(pair + step) % pairs for step in range(1, pairs)]
    pair_sources = [(pair + pairs - step) % pairs for step in range(1, pairs)]
    across = [{"fsdp": peer * 2 + core, "seq": line} for peer in pair_peers]
    half_peers = [(half + step) % halves for step in range(1, halves)]
    along = [{"fsdp": place, "seq": peer * 2 + side} for peer in half_peers]
    seq_peers = [{"fsdp": place, "seq": (line + step) % size} for step in range(1, size)]
    later, earlier = seq_peers[0], seq_peers[-1]

    used = [0]
    started = []

    def send(source, target, device):
        slot = used[0]
        used[0] += 1
        copy = pltpu.make_async_remote_copy(
            src_ref=source,
            dst_ref=target,
            send_sem=send_sem.at[slot],
            recv_sem=recv_sem.at[slot],
            device_id=device,
            device_id_type=mesh_id,
        )
        copy.start()
        started.append(copy)
        return copy

    small[place] = jnp.zeros(small.shape[1:], F32)
    for at, vector in enumerate((gain_a, offset_a, gain_b, offset_b)):
        small[place, at : at + 1, :part] = vector[...].astype(F32)
    table_rows = table.shape[0]
    small[place, 4 : 4 + table_rows, : d.entries] = table[...].astype(F32)

    barrier = pltpu.get_barrier_semaphore()
    greeted = [partner] + across + seq_peers
    for device in greeted:
        pl.semaphore_signal(barrier, inc=1, device_id=device, device_id_type=mesh_id)
    pl.semaphore_wait(barrier, len(greeted))

    pieces = []
    for at, count in enumerate((1, 1, 2, 2)):
        rows, columns = weights[at].shape[1:]
        for step in range(count):
            if columns // count % 128:
                where = (pl.ds(step * (rows // count), rows // count), slice(None))
            else:
                where = (slice(None), pl.ds(step * (columns // count), columns // count))
            pieces.append((at,) + where)
    far, near, home, kept = {}, {}, {}, {}

    def gather_far(index):
        at, rows, columns = pieces[index]
        for step, device in enumerate(across):
            source = weights[at].at[side, rows, columns]
            far[index, step] = send(source, fulls[at].at[place, side, rows, columns], device)

    def gather_near(index):
        at, rows, columns = pieces[index]
        for step, source in enumerate(pair_sources):
            far[index, step].wait_recv()
            came = fulls[at].at[source * 2 + core, side, rows, columns]
            near[index, step] = send(came, came, beside)
        if index + window_far < len(pieces):
            gather_far(index + window_far)

    def gather_home(index):
        at, rows, columns = pieces[index]
        for step, source in enumerate(pair_sources):
            near[index, step].wait_recv()
            came = fulls[at].at[source * 2 + core, :, rows, columns]
            home.setdefault(at, []).append(send(came, came, partner))

    window_far = 4
    gathers = sorted(
        (index + 2 * lag, lag, index) for index in range(len(pieces)) for lag in range(2)
    )

    def gather(count):
        for _ in range(min(count, len(gathers))):
            _, lag, index = gathers.pop(0)
            (gather_home if lag else gather_near)(index)

    def gather_done(at):
        last_piece = max(index for index, piece in enumerate(pieces) if piece[0] == at)
        while any(lag == 1 and index <= last_piece for _, lag, index in gathers):
            gather(1)
        for copy in home[at]:
            copy.wait_recv()
        kept[at].wait()

    own_small = small.at[place]
    small_far = [send(own_small, own_small, device) for device in across]
    small_home = [send(own_small, own_small, partner)]
    for index in range(window_far):
        gather_far(index)
    halo_copies = [send(tok.at[0, 0:SHIFT], halo_tok, earlier)]
    halo_copies.append(send(cot.at[0, 0:SHIFT], halo_cot, earlier))
    for at in range(len(weights)):
        home[at] = [send(weights[at], fulls[at].at[place], partner)]
        kept[at] = pltpu.make_async_copy(weights[at], fulls[at].at[place], copy_sem.at[at])
        kept[at].start()

    def token_of(slot_at):
        row, col, real = place_of(slot_at, d.num_cols)
        token_col = jnp.where(col + SHIFT >= d.num_cols, col + SHIFT - d.num_cols, col + SHIFT)
        return jnp.where(real, row * d.stride + token_col, -1)

    hit = iota((d.slots, d.natural), 1) == token_of(iota((d.slots, 1), 0))
    perm[...] = jnp.where(hit, 1.0, 0.0).astype(LOW)
    hit = iota((d.natural, d.slots), 0) == token_of(iota((1, d.slots), 1))
    perm_t[...] = jnp.where(hit, 1.0, 0.0).astype(LOW)
    span = d.per_group * SLOT
    block_down = divide(iota((span, 1), 0), SLOT)
    hit = block_down == divide(iota((1, LANES), 1), d.head_dim)
    heads[...] = jnp.where(hit, 1.0, 0.0).astype(LOW)
    hit = block_down == divide(iota((1, span), 1), SLOT)
    ones[...] = jnp.where(hit, 1.0, 0.0).astype(LOW)

    grid_cols, grid_rows = reg.shape
    row, col, real = place_of(iota((d.slots, 1), 0), d.num_cols)
    picked = jnp.where(iota((d.slots, grid_rows), 1) == line * d.num_rows + row, 1.0, 0.0)
    by_row = nt(picked.astype(LOW), reg[...].astype(F32).astype(LOW))
    regions = jnp.sum(
        jnp.where(iota((d.slots, grid_cols), 1) == col, by_row, 0.0), axis=1, keepdims=True
    )
    regions_t = jnp.transpose(jnp.broadcast_to(regions, (d.slots, 128)))
    for window in range(d.windows):
        down = regions[window * SLOT : (window + 1) * SLOT]
        over = regions_t[0:1, window * SLOT : (window + 1) * SLOT]
        added = jnp.where(down == over, 0.0, MASKED).astype(F32)
        mask[window] = jnp.concatenate([added, added], axis=1)

    positions = rel.shape[0]
    rel_pad[...] = jnp.full(rel_pad.shape, -1.0, F32)
    rel_pad[:positions, :positions] = rel[...].astype(F32)
    rel_pad[...] = jnp.transpose(rel_pad[...])
    table_lanes = small.shape[2]

    rel_t = rel_pad[:SLOT]
    for at in range(onehot.shape[0]):
        hit = rel_t[:, at : at + 1] == iota((1, table_lanes), 1).astype(F32)
        onehot[at] = jnp.where(hit, 1.0, 0.0).astype(LOW)

    natural[...] = jnp.zeros(natural.shape, LOW)
    keep = d.num_rows - SHIFT

    def windowed(field, halo, copy):
        copy.wait_recv()
        for at in range(d.num_rows):
            source = field[0, at + SHIFT] if at < keep else halo[at - keep]
            natural[at * d.stride : at * d.stride + d.num_cols] = source
        return nn(perm[...], natural[...])

    inputs = windowed(tok, halo_tok, halo_copies[0])

    for step, source in enumerate(pair_sources):
        small_far[step].wait_recv()
        came = small.at[source * 2 + core]
        small_home.append(send(came, came, partner))
    for copy in small_home:
        copy.wait_recv()

    def vector_of(at):
        return jnp.concatenate([small[owner, at : at + 1, :part] for owner in range(owners)], axis=1)

    norm_gain_a, norm_offset_a, norm_gain_b, norm_offset_b = [vector_of(at) for at in range(4)]
    normed, normed_hat, inverse_a = layer_norm(inputs, norm_gain_a, norm_offset_a)
    hat_a[...] = normed_hat
    low_a[...] = normed.astype(LOW)

    def by_owner(values):
        rows = values.shape[0] // owners
        return values.reshape(pairs, 2, rows, values.shape[1])

    at_a[...] = by_owner(jnp.transpose(low_a[...]))
    swaps = {}
    swaps["a"] = send(at_a.at[:, 1 - core], at_a_in, partner)
    gather(2)

    whole_table = jnp.concatenate(
        [small[owner, 4 : 4 + table_rows] for owner in range(owners)], axis=0
    ).astype(LOW)

    batch = LANES // SLOT
    for step in range(onehot.shape[0] // batch):
        picks = onehot[step * batch : (step + 1) * batch].reshape(batch * SLOT, table_lanes)
        found = nt(whole_table, picks)
        for at in range(batch):
            spread[pl.ds(step * batch + at, d.num_heads, stride=SLOT), :SLOT] = found[:, at * SLOT : (at + 1) * SLOT]

    removed = jnp.where(iota((SLOT, SLOT), 1) < WS * WS, 0.0, REMOVED)
    for head in range(0, d.num_heads, 2):
        one = spread[head * SLOT : (head + 1) * SLOT, :SLOT] + removed
        two = spread[(head + 1) * SLOT : (head + 2) * SLOT, :SLOT] + removed
        bias[:, head * SLOT : (head + 2) * SLOT] = jnp.concatenate([one, two], axis=1)

    gather(1)
    g_cot[0] = windowed(cot, halo_cot, halo_copies[1]).astype(LOW)
    swaps["cot"] = send(g_cot.at[0], g_cot.at[1], partner)
    gather_done(0)

    def weight(at, cols):
        values = fulls[at][:, :, :, cols]
        return values.reshape(-1, values.shape[-1])

    scale = d.head_dim ** (-0.5)
    for at in range(3):
        columns = pl.ds(at * width, width)
        values = nn(low_a[...], weight(0, columns))
        qkv[at] = (values * scale if at == 0 else values).astype(LOW)

    def span_of(window, group):
        return pl.ds(window * SLOT, SLOT), pl.ds(group * LANES, LANES)

    def blocks_of(tile):
        return jnp.concatenate([tile] * d.per_group, axis=0) * heads[...]

    for window in range(d.windows):
        for group in range(d.groups):
            rows, lanes = span_of(window, group)
            scores = nt(qkv[0, rows, lanes], blocks_of(qkv[1, rows, lanes]))
            scores += bias[:, group * span : (group + 1) * span]
            scores += jnp.concatenate([mask[window]] * (d.per_group // 2), axis=1)
            powers = jnp.exp(scores)
            share = powers / sum_exact(powers, ones[...])
            probs[window, group] = share
            found = nn(share.astype(LOW), blocks_of(qkv[2, rows, lanes]))
            attended[rows, lanes] = found.astype(LOW)
        gather(2 if window < 2 else 1)
    at_c[...] = by_owner(jnp.transpose(attended[...]))
    swaps["c"] = send(at_c.at[:, 1 - core], at_c_in, partner)
    gather_done(1)
    middle[...] = inputs + nn(attended[...], weight(1, slice(None)))
    normed, normed_hat, inverse_b = layer_norm(middle[...], norm_gain_b, norm_offset_b)
    hat_b[...] = normed_hat
    low_b = normed.astype(LOW)
    at_b[...] = by_owner(jnp.transpose(low_b))
    swaps["b"] = send(at_b.at[:, 1 - core], at_b_in, partner)
    gather_done(2)

    tile_owners = owners // d.tiles
    for tile in range(d.tiles):
        columns = pl.ds(tile * width, width)
        hidden = nn(low_b, weight(2, columns))
        activated, slope_tile = gelu_parts(hidden)
        slope[tile] = slope_tile
        act_low = activated.astype(LOW)
        act[:, tile * width : (tile + 1) * width] = act_low
        turned = jnp.transpose(act_low).reshape(tile_owners, -1, d.slots)
        for at in range(tile_owners):
            owner = tile * tile_owners + at
            at_d[owner // 2, owner % 2] = turned[at]
            if owner % 2:
                pair_at = owner // 2
                copy = send(at_d.at[pair_at, 1 - core], at_d_in.at[pair_at], partner)
                swaps["d", pair_at] = copy

    stage_copies = {}

    def reduce_start(block, own, came, right, came_right):
        own, came = own.reshape(-1, d.slots), came.reshape(-1, d.slots)
        for step in range(CUTS):
            chunk, columns = block * CUTS + step, slice(step * d.cut, (step + 1) * d.cut)
            total = nn(own, right[:, columns]) + nn(came, came_right[:, columns])
            grads[chunk] = total.astype(LOW).reshape(grads.shape[1:])
            stage_copies[chunk, 0] = [
                send(grads.at[chunk, peer], in_two.at[chunk, at], device)
                for at, (peer, device) in enumerate(zip(pair_peers, across))
            ]

    def wide(ref, *index):
        return ref[index].astype(F32)

    def stage_two(chunk):
        total = wide(grads, chunk, pair)
        for step in range(pairs - 1):
            total += wide(in_two, chunk, step)
        sum_two[chunk] = total.astype(LOW)
        return [send(sum_two.at[chunk, 1 - side], in_three.at[chunk], beside)]

    def stage_three(chunk):
        total = (wide(sum_two, chunk, side) + wide(in_three, chunk)).astype(LOW)
        sum_three[chunk] = total
        if d.scatter:
            return [
                send(sum_three.at[chunk, peer], in_four.at[chunk, step], device)
                for step, (peer, device) in enumerate(zip(half_peers, along))
            ]
        in_four[chunk, half] = total[0]
        mine = in_four.at[chunk, half]
        return [send(sum_three.at[chunk, 0], mine, device) for device in along]

    def stage_four(chunk):
        if d.scatter:
            total = wide(sum_three, chunk, half)
            for step in range(halves - 1):
                total += wide(in_four, chunk, step)
            result[chunk, side, half] = total.astype(LOW)
            mine = result.at[chunk, side, half]
            return [send(mine, mine, device) for device in along]
        total = wide(in_four, chunk, 0)
        for at in range(1, halves):
            total += wide(in_four, chunk, at)
        result[chunk, side, 0] = total.astype(LOW)
        return []

    def stage_five(chunk):
        mine = result.at[chunk, side]
        return [send(mine, mine, beside)]

    def stage_six(chunk):
        return []

    stages = (stage_two, stage_three, stage_four, stage_five, stage_six)
    events = sorted(
        (chunk + SPREAD * lag, lag, chunk) for chunk in range(d.chunks) for lag in range(len(stages))
    )

    def advance(limit):
        while events and events[0][0] <= limit:
            _, lag, chunk = events.pop(0)
            for copy in stage_copies[chunk, lag]:
                copy.wait_recv()
            stage_copies[chunk, lag + 1] = stages[lag](chunk)

    swaps["cot"].wait_recv()
    for pair_at in range(pairs):
        swaps["d", pair_at].wait_recv()
    for chunk in range(d.tiles):
        rows = pl.ds(chunk * part, part)
        reduce_start(chunk, at_d[:, core, rows], at_d_in[:, rows], g_cot[0], g_cot[1])

    gather_done(3)
    for tile in range(d.tiles):
        whole = fulls[3][tile * tile_owners : (tile + 1) * tile_owners].reshape(width, width)
        hidden_grad = (nt(g_cot[0], whole) * slope[tile]).astype(LOW)
        g_hid[tile, 0] = hidden_grad
        swaps["h", tile] = send(g_hid.at[tile, 0], g_hid.at[tile, 1], partner)
        term = nt(hidden_grad, weight(2, pl.ds(tile * width, width)))
        upstream_two = term if tile == 0 else upstream_two + term
    swaps["b"].wait_recv()
    for tile in range(d.tiles):
        swaps["h", tile].wait_recv()
        reduce_start(d.tiles + tile, at_b[:, core], at_b_in[...], g_hid[tile, 0], g_hid[tile, 1])

    out_tiles = (middle[...] + nn(act[...], fulls[3][...].reshape(-1, width))).astype(LOW)
    out_rows = nn(perm_t[...], out_tiles).astype(LOW)
    for at in range(d.num_rows):
        field = out_rows[at * d.stride : at * d.stride + d.num_cols]
        if at < keep:
            out[0, at + SHIFT] = field
        else:
            halo_out[at - keep] = field
    last = [send(halo_out, out.at[0, 0:SHIFT], later)]

    advance(1)
    back_two, gain_b_grad, offset_b_grad = norm_back(upstream_two, hat_b[...], inverse_b, norm_gain_b)
    middle_grad = g_cot[0].astype(F32) + back_two
    middle_low = middle_grad.astype(LOW)
    g_mid[0] = middle_low
    swaps["m"] = send(g_mid.at[0], g_mid.at[1], partner)
    attended[...] = nt(middle_low, weight(1, slice(None))).astype(LOW)
    middle[...] = middle_grad
    swaps["m"].wait_recv()
    swaps["c"].wait_recv()
    reduce_start(2 * d.tiles, at_c[:, core], at_c_in[...], g_mid[0], g_mid[1])
    advance(2)

    def fold(values):
        kept_lanes = values * heads[...].astype(F32)
        return jnp.sum(kept_lanes.reshape(d.per_group, SLOT, LANES), axis=0)

    for window in range(d.windows):
        for group in range(d.groups):
            rows, lanes = span_of(window, group)
            query, key, value = [qkv[at, rows, lanes] for at in range(3)]
            keys = blocks_of(key)
            share = probs[window, group]
            given = attended[rows, lanes]
            prob_grad = nt(given, blocks_of(value))
            inner = sum_exact(share * prob_grad, ones[...])
            score_grad = share * (prob_grad - inner)
            score_low = score_grad.astype(LOW)
            across_heads = slice(group * span, (group + 1) * span)
            if window == 0:
                bias[:, across_heads] = score_grad
            else:
                bias[:, across_heads] += score_grad
            g_qkv[0, 0, rows, lanes] = (nn(score_low, keys) * scale).astype(LOW)
            g_qkv[1, 0, rows, lanes] = fold(tn(score_low, query)).astype(LOW)
            g_qkv[2, 0, rows, lanes] = fold(tn(share.astype(LOW), given)).astype(LOW)
        advance(3 + window)

    for at in range(3):
        swaps["q", at] = send(g_qkv.at[at, 0], g_qkv.at[at, 1], partner)
    swaps["a"].wait_recv()
    for at in range(3):
        term = nt(g_qkv[at, 0], weight(0, pl.ds(at * width, width)))
        upstream_one = term if at == 0 else upstream_one + term
        swaps["q", at].wait_recv()
        reduce_start(2 * d.tiles + 1 + at, at_a[:, core], at_a_in[...], g_qkv[at, 0], g_qkv[at, 1])
    advance(7)

    back_one, gain_a_grad, offset_a_grad = norm_back(upstream_one, hat_a[...], inverse_a, norm_gain_a)

    for head in range(d.num_heads):
        spread[head * SLOT : (head + 1) * SLOT, :SLOT] = bias[:, head * SLOT : (head + 1) * SLOT]

    for step in range(onehot.shape[0] // batch):
        pieces = [
            spread[pl.ds(step * batch + at, d.num_heads, stride=SLOT), :SLOT] for at in range(batch)
        ]
        high, low = split(jnp.concatenate(pieces, axis=1))
        picks = onehot[pl.ds(step * batch, batch)].reshape(batch * SLOT, table_lanes)
        table_sum[step] = nn(jnp.concatenate([high, low], axis=0), picks)

    table_total = jnp.sum(table_sum[...], axis=0)
    table_grad = table_total[: d.num_heads] + table_total[d.num_heads :]
    small_grad[...] = jnp.zeros(small_grad.shape, F32)
    vector_grads = (gain_a_grad, offset_a_grad, gain_b_grad, offset_b_grad)
    for owner in range(owners):
        spot = (owner // 2, owner % 2)
        for at, vector in enumerate(vector_grads):
            small_grad[spot + (slice(at, at + 1), slice(0, part))] = vector[:, owner * part : (owner + 1) * part]
        rows = table_grad[owner * table_rows : (owner + 1) * table_rows]
        small_grad[spot + (slice(4, 4 + table_rows),)] = rows
    small_home = send(small_grad.at[:, 1 - core], small_in, partner)
    advance(8)

    final = middle[...] + back_one
    high, low = split(final)
    final_rows = nn(perm_t[...], high) + nn(perm_t[...], low)
    for at in range(d.num_rows):
        field = final_rows[at * d.stride : at * d.stride + d.num_cols]
        if at < keep:
            tok_grad[0, at + SHIFT] = field
        else:
            halo_grad[at - keep] = field.astype(LOW)
    grad_copy = send(halo_grad, came_grad, later)

    small_home.wait_recv()
    small_sum[...] = small_grad[:, core] + small_in[...]
    small_far = [
        send(small_sum.at[peer], small_two.at[step], device)
        for step, (peer, device) in enumerate(zip(pair_peers, across))
    ]
    advance(9)
    total = small_sum[pair]
    for step in range(pairs - 1):
        small_far[step].wait_recv()
        total += small_two[step]
    small_all[line] = total
    mine = small_all.at[line]
    small_copies = [send(mine, mine, device) for device in seq_peers]
    advance(d.chunks + 2)
    grad_copy.wait_recv()
    for at in range(SHIFT):
        tok_grad[0, at] = came_grad[at].astype(F32)
    for copy in small_copies:
        copy.wait_recv()
    total = small_all[0]
    for at in range(1, size):
        total += small_all[at]
    for at, target in enumerate((d_gain_a, d_offset_a, d_gain_b, d_offset_b)):
        target[...] = total[at : at + 1, :part]
    d_table[...] = total[4 : 4 + table_rows, : d.entries]
    advance(d.chunks + SPREAD * len(stages))

    for copy in last:
        copy.wait_recv()
    for copy in started:
        copy.wait_send()


def pass_on(d, *refs):
    sources, targets = refs[:8], refs[8:]
    for at, (source, target) in enumerate(zip(sources[:7], targets[:7])):
        target[...] = source[0].reshape(target.shape) if at == 1 else source[...]
    totals, (qkv, proj, expand, reduce) = sources[7], targets[7:]
    for chunk in range(d.chunks):
        total = totals[chunk].astype(F32).reshape(d.part, d.cut)
        block, step = chunk // CUTS, chunk % CUTS
        if block < d.tiles:
            reduce[block * d.part : (block + 1) * d.part, step * d.cut : (step + 1) * d.cut] = total
            continue
        if block < 2 * d.tiles:
            target, start = expand, chunk - d.tiles * CUTS
        elif block == 2 * d.tiles:
            target, start = proj, step
        else:
            target, start = qkv, chunk - (2 * d.tiles + 1) * CUTS
        target[:, start * d.cut : (start + 1) * d.cut] = total


def shards(
    tokens,
    cotangent,
    region_ids,
    relative_index,
    first_gain,
    first_offset,
    qkv_weight,
    proj_weight,
    bias_table,
    second_gain,
    second_offset,
    expand_weight,
    reduce_weight,
):
    owners = lax.axis_size("fsdp")
    size = lax.axis_size("seq")
    _, num_rows, num_cols, width = tokens.shape
    table_rows, entries = bias_table.shape
    hidden = expand_weight.shape[1]
    num_heads = table_rows * owners
    d = Dims(owners, size, num_rows, num_cols, width, hidden, num_heads, entries)
    pairs, halves, part = d.pairs, d.halves, d.part
    slots, span = d.slots, d.per_group * SLOT
    weights = [
        weight.reshape(2, weight.shape[0] // 2, weight.shape[1])
        for weight in (qkv_weight, proj_weight, expand_weight, reduce_weight)
    ]
    vectors = [
        vector.reshape(1, part) for vector in (first_gain, first_offset, second_gain, second_offset)
    ]
    entry_lanes = -(-entries // 128) * 128
    small_rows = -(-(4 + table_rows) // 8) * 8
    held = -(-WS * WS // 4) * 4
    chunks, fine, piece = d.chunks, d.fine, d.piece
    hidden_part = hidden // owners

    def low(*shape):
        return pltpu.VMEM(shape, LOW)

    def full(*shape):
        return pltpu.VMEM(shape, F32)

    scratch = [low(owners, *weight.shape) for weight in weights]
    scratch += [
        full(owners, small_rows, entry_lanes),
        low(SHIFT, num_cols, width),
        low(SHIFT, num_cols, width),
        low(SHIFT, num_cols, width),
        low(SHIFT, num_cols, width),
        low(SHIFT, num_cols, width),
        low(d.natural, width),
        full(slots, width),
        full(slots, width),
        full(slots, width),
        low(slots, width),
    ]
    scratch += [
        low(3, slots, width),
        full(d.windows, d.groups, SLOT, span),
        low(slots, width),
        full(d.tiles, slots, width),
        low(slots, hidden),
        low(slots, d.natural),
        low(d.natural, slots),
        low(span, LANES),
        low(span, span),
        low(held, SLOT, entry_lanes),
        full(128, 128),
        full(SLOT, num_heads * SLOT),
        full(num_heads * SLOT, 128),
        full(d.windows, SLOT, 2 * SLOT),
    ]
    for rows in (part, part, part, hidden_part):
        scratch += [low(pairs, 2, rows, slots), low(pairs, rows, slots)]
    scratch += [
        low(2, slots, width),
        low(d.tiles, 2, slots, width),
        low(2, slots, width),
        low(3, 2, slots, width),
    ]
    scratch += [
        low(chunks, pairs, 2, fine, piece, d.cut),
        low(chunks, max(pairs - 1, 1), 2, fine, piece, d.cut),
        low(chunks, 2, fine, piece, d.cut),
        low(chunks, fine, piece, d.cut),
        low(chunks, fine, piece, d.cut),
        low(chunks, halves, piece, d.cut),
        full(pairs, 2, small_rows, entry_lanes),
        full(pairs, small_rows, entry_lanes),
        full(pairs, small_rows, entry_lanes),
        full(max(pairs - 1, 1), small_rows, entry_lanes),
        full(size, small_rows, entry_lanes),
        full(held * SLOT // LANES, 2 * num_heads, entry_lanes),
    ]
    scratch += [pltpu.SemaphoreType.DMA((d.copies,))] * 2
    scratch += [pltpu.SemaphoreType.DMA((len(weights),))]

    def shape(*dims):
        return jax.ShapeDtypeStruct(dims, F32)

    in_vmem = pl.BlockSpec(memory_space=pltpu.VMEM)
    outs = pl.pallas_call(
        functools.partial(body, d),
        out_shape=[
            jax.ShapeDtypeStruct(tokens.shape, LOW),
            shape(*tokens.shape),
            shape(1, part),
            shape(1, part),
            shape(table_rows, entries),
            shape(1, part),
            shape(1, part),
            jax.ShapeDtypeStruct((chunks, 2, fine, piece, d.cut), LOW),
        ],
        in_specs=[in_vmem] * 13,
        out_specs=[in_vmem] * 8,
        scratch_shapes=scratch,
        compiler_params=pltpu.CompilerParams(
            collective_id=0, has_side_effects=True, vmem_limit_bytes=60 * 1024 * 1024
        ),
    )(tokens, cotangent, region_ids.T, relative_index, *vectors, bias_table, *weights)
    shapes = [jax.ShapeDtypeStruct(o.shape, o.dtype) for o in outs[:-1]]
    shapes[1] = shape(num_rows, num_cols, 1, width)
    shapes += [shape(part, 3 * width), shape(part, width), shape(part, hidden), shape(hidden_part, width)]
    outs = pl.pallas_call(
        functools.partial(pass_on, d),
        out_shape=shapes,
        in_specs=[in_vmem] * 8,
        out_specs=[in_vmem] * len(shapes),
        compiler_params=pltpu.CompilerParams(vmem_limit_bytes=60 * 1024 * 1024),
    )(*outs)
    out, tok_grad, gain_a, offset_a, table_grad, gain_b, offset_b, qkv, proj, expand, reduce = outs
    gain_a, offset_a, gain_b, offset_b = [o.reshape(part) for o in (gain_a, offset_a, gain_b, offset_b)]
    tok_grad = tok_grad.reshape(tokens.shape)
    return out, tok_grad, gain_a, offset_a, qkv, proj, table_grad, gain_b, offset_b, expand, reduce


def solution(mesh):
    rows, vector, grid = P("fsdp", None), P("fsdp"), P("fsdp", "seq", None, None)
    return jax.shard_map(
        shards,
        mesh=mesh,
        in_specs=(grid, grid, P(), P(), vector, vector, rows, rows, rows, vector, vector, rows, rows),
        out_specs=(grid, grid, vector, vector, rows, rows, rows, vector, vector, rows, rows),
        check_vma=False,
    )
```
